32 devices in a mesh: dp: 4 (over z), tensor: 4 (over y, x), seq: 2 (over core).
Axes of the slice: x: 2, y: 2, z: 4, core: 2. Of those that a mesh axis runs over, the one named last changes fastest.
Arguments:
- hidden: bfloat16 [1024, 4096], P(('dp', 'seq'), 'tensor'), may hold values from -6 to 6
- w_in: bfloat16 [4096, 512], P('tensor'), may hold values from -0.09375 to 0.09375
- embed: bfloat16 [1024, 512], replicated, may hold values from -16 to 16
- gain: float32 [512], replicated, may hold values from 0.1 to 1.9
- w_head: bfloat16 [512, 1024], replicated, may hold values from -2 to 2
- tokens: int32 [1024, 8], P(('dp', 'seq')), may hold values from 0 to 1023
- frame_mask: int32 [1024], P(('dp', 'seq')), may hold values from 0 to 1, as said below
Outputs:
- loss: float32 [], replicated
- grad_head: float32 [524288], P(('dp', 'tensor', 'seq'))
- grad_hidden: bfloat16 [1024, 4096], P(('dp', 'seq'), 'tensor')
The draws below stay inside these ranges and needn't reach their ends.
Inputs may be any that keep to these rules, and one draw needn't show every extreme that they name: `frame_mask`: frame 0 always counts.
All inputs are finite; a program needn't handle non-finite values.
Results may differ from the reference program's by a relative error of at most 0.015.
Values may be sent and summed in bfloat16 or wider, within the bound.
A program may use at most 64 MiB of HBM per device.

```python
import jax
import jax.numpy as jnp
from jax import lax

D = 4096
DD = 512
V = 1024
K = 8
FR_DEV = 32
FRAMES = 1024
N_TENSOR = 4


def draw_embed(key, part):
    base = jnp.clip(jax.random.normal(jax.random.fold_in(key, 1), (V, DD), jnp.float32), -6.0, 6.0)
    return base.astype(jnp.bfloat16)


def draw_w_head(key, part):
    base = jax.random.normal(jax.random.fold_in(key, 4), (DD, V), jnp.float32) * DD ** (-0.5)
    return base.astype(jnp.bfloat16)


def draw_frame_mask(key, part):
    place = jnp.arange(FRAMES, dtype=jnp.int32)
    levels = jax.random.randint(key, (FRAMES,), 0, 1000)
    limit = 300 + 600 * (place // max(FRAMES // 1000, 1)) // max(FRAMES // max(FRAMES // 1000, 1), 1)
    counted = (levels < limit).astype(jnp.int32)
    return counted.at[0].set(1)


def place_ends(values, own_key, least, high):
    spot = [jax.random.randint(jax.random.fold_in(own_key, axis), (), 0, length) for axis, length in enumerate(values.shape)]
    widest = values.shape.index(max(values.shape))
    beside = spot[:widest] + [(spot[widest] + 1) % values.shape[widest]] + spot[widest + 1:]
    return values.at[tuple(spot)].set(least).at[tuple(beside)].set(high)


def shard_levels(stream_key, shape, cuts, low, high):
    def one(position, parts):
        draws = jax.random.uniform(jax.random.fold_in(jax.random.fold_in(stream_key, 6), position), (parts,), jnp.float32, low / len(cuts), high / len(cuts))
        return jnp.repeat(jnp.exp(draws), shape[position] // parts).reshape((-1,) + (1,) * (len(shape) - position - 1))

    factor_of = one(*cuts[0])
    for cut in cuts[1:]:
        factor_of = factor_of * one(*cut)
    return factor_of


def bell_draw(rng, dims, scale, reach, shards=(), kind=jnp.bfloat16):
    entries = scale * jax.random.normal(rng, dims, jnp.float32)
    if shards:
        entries = entries * shard_levels(rng, dims, shards, -0.22, 0.18)
    return jnp.clip(entries, -reach, reach).astype(kind)


def setup_inputs(seed: int = 0) -> dict:
    key_list = jax.random.split(jax.random.key(seed), 8)
    hidden = bell_draw(key_list[0], (FRAMES, D), 1.0, 6.0, ((0, 8), (1, 4)))
    w_in = bell_draw(key_list[1], (D, DD), D ** -0.5, 0.09375, ((0, 4),))
    embed = draw_embed(jax.random.fold_in(key_list[7], 71), 0)
    gain = jnp.clip(1.0 + 0.18 * jax.random.normal(key_list[3], (DD,), jnp.float32), 0.1, 1.9)
    w_head = draw_w_head(jax.random.fold_in(key_list[7], 71), 0)
    tokens = place_ends(jax.random.randint(key_list[5], (FRAMES, K), 0, V), jax.random.fold_in(key_list[5], 1), 0, V - 1).astype(jnp.int32)
    frame_mask = draw_frame_mask(jax.random.fold_in(key_list[7], 71), 0)
    return dict(hidden=hidden, w_in=w_in, embed=embed, gain=gain, w_head=w_head, tokens=tokens, frame_mask=frame_mask)


def block_terms(hblk, tblk, mblk, w_in, embed, gain, w_head, count):
    context = jnp.dot(hblk, w_in, preferred_element_type=jnp.float32).astype(jnp.bfloat16)
    frames = context.shape[0]
    width = context.shape[1]
    steps = tblk.shape[1]
    before = embed[tblk[:, :-1]].astype(jnp.float32)
    leading = jnp.zeros((frames, 1, width), jnp.float32)
    inputs = context.astype(jnp.float32)[:, None, :] + jnp.concatenate([leading, before], 1)
    inverse = lax.rsqrt(lax.optimization_barrier(jnp.mean(inputs * inputs, -1, keepdims=True)) + 1e-06)
    normed = inputs * inverse
    scaled = (normed * gain).astype(jnp.bfloat16)
    flat = scaled.reshape(frames * steps, width)
    logits = jnp.dot(flat, w_head, preferred_element_type=jnp.float32)
    top = lax.optimization_barrier(jnp.max(logits, -1, keepdims=True))
    total = top[:, 0] + jnp.log(lax.optimization_barrier(jnp.sum(jnp.exp(logits - top), -1)))
    target = tblk.reshape(-1)
    onehot = (target[:, None] == jnp.arange(w_head.shape[1], dtype=jnp.int32)[None, :]).astype(jnp.float32)
    nll = total - lax.optimization_barrier(jnp.sum(logits * onehot, -1))
    weights = (mblk.astype(jnp.float32)[:, None] * jnp.ones((1, steps), jnp.float32)).reshape(-1)
    loss_part = jnp.sum(weights * nll)
    probs = jnp.exp(logits - total[:, None])
    grad_logits = ((probs - onehot) * weights[:, None] / count).astype(jnp.bfloat16)
    head_term = lax.dot_general(flat, grad_logits, (((0,), (0,)), ((), ())), preferred_element_type=jnp.float32)
    grad_scaled = lax.dot_general(grad_logits, w_head, (((1,), (1,)), ((), ())), preferred_element_type=jnp.float32)
    scaled_grad = grad_scaled.reshape(inputs.shape) * gain
    grad_inputs = inverse * (scaled_grad - normed * lax.optimization_barrier(jnp.mean(scaled_grad * normed, -1, keepdims=True)))
    grad_context = lax.optimization_barrier(jnp.sum(grad_inputs, 1)).astype(jnp.bfloat16)
    return (loss_part, head_term, grad_context)

def reference(hidden, w_in, embed, gain, w_head, tokens, frame_mask):
    count = K * jnp.sum(frame_mask.astype(jnp.float32))
    block = N_TENSOR * FR_DEV
    blocks = hidden.shape[0] // block

    def advance(carry, pieces):
        loss_sum, head = carry
        hblk, tblk, mblk = pieces
        loss_part, head_term, grad_context = block_terms(hblk, tblk, mblk, w_in, embed, gain, w_head, count)
        grad_h = lax.dot_general(grad_context, w_in, (((1,), (1,)), ((), ())), preferred_element_type=jnp.float32).astype(jnp.bfloat16)
        return ((loss_sum + loss_part, head + head_term), grad_h)
    start = (jnp.zeros((), jnp.float32), jnp.zeros((w_head.shape[0], w_head.shape[1]), jnp.float32))
    pieces = (hidden.reshape(blocks, block, hidden.shape[1]), tokens.reshape(blocks, block, tokens.shape[1]), frame_mask.reshape(blocks, block))
    (loss_sum, head), grad_h = lax.scan(advance, start, pieces)
    return (loss_sum / count, head.reshape(-1), grad_h.reshape(hidden.shape))
```

```python
import functools

import jax
import jax.numpy as jnp
from jax import lax
from jax.experimental import pallas as pl
from jax.experimental.pallas import tpu as pltpu
from jax.sharding import PartitionSpec as P

F32 = jnp.float32
BF16 = jnp.bfloat16
MESH = pl.DeviceIdType.MESH


def decode_terms(context, tok_rows, mask_rows, embed, gain, w_head, count_fn):
    frames = context.shape[0]
    width = context.shape[1]
    steps = tok_rows.shape[1]
    before = embed[tok_rows[:, :-1]].astype(jnp.float32)
    leading = jnp.zeros((frames, 1, width), jnp.float32)
    inputs = context.astype(jnp.float32)[:, None, :] + jnp.concatenate([leading, before], 1)
    inverse = lax.rsqrt(jnp.mean(inputs * inputs, -1, keepdims=True) + 1e-06)
    normed = inputs * inverse
    scaled = (normed * gain).astype(jnp.bfloat16)
    flat = scaled.reshape(frames * steps, width)
    logits = jnp.dot(flat, w_head, preferred_element_type=jnp.float32)
    top = jnp.max(logits, -1, keepdims=True)
    total = top[:, 0] + jnp.log(jnp.sum(jnp.exp(logits - top), -1))
    target = tok_rows.reshape(-1)
    onehot = (target[:, None] == jnp.arange(w_head.shape[1], dtype=jnp.int32)[None, :]).astype(
        jnp.float32
    )
    nll = total - jnp.sum(logits * onehot, -1)
    weights = (mask_rows.astype(jnp.float32)[:, None] * jnp.ones((1, steps), jnp.float32)).reshape(
        -1
    )
    count, loss_sum = count_fn(
        steps * jnp.sum(mask_rows.astype(jnp.float32)), jnp.sum(weights * nll)
    )
    probs = jnp.exp(logits - total[:, None])
    grad_logits = ((probs - onehot) * weights[:, None] / count).astype(jnp.bfloat16)
    head_term = lax.dot_general(
        flat, grad_logits, (((0,), (0,)), ((), ())), preferred_element_type=jnp.float32
    )
    grad_scaled = lax.dot_general(
        grad_logits, w_head, (((1,), (1,)), ((), ())), preferred_element_type=jnp.float32
    )
    scaled_grad = grad_scaled.reshape(inputs.shape) * gain
    grad_inputs = inverse * (
        scaled_grad - normed * jnp.mean(scaled_grad * normed, -1, keepdims=True)
    )
    grad_context = jnp.sum(grad_inputs, 1).astype(jnp.bfloat16)
    return (loss_sum / count, head_term, grad_context)


def add_totals(count_local, loss_local):
    return lax.psum((count_local, loss_local), ("dp", "tensor", "seq"))


def per_device_plain(hidden, w_in, embed, gain, w_head, tokens, frame_mask):
    groups = lax.axis_size("tensor")
    rows = hidden.shape[0] // groups
    context = lax.psum_scatter(
        jnp.dot(hidden, w_in, preferred_element_type=jnp.float32),
        "tensor",
        scatter_dimension=0,
        tiled=True,
    ).astype(jnp.bfloat16)
    offset = lax.axis_index("tensor") * rows
    tok_rows = lax.dynamic_slice_in_dim(tokens, offset, rows, 0)
    mask_rows = lax.dynamic_slice_in_dim(frame_mask, offset, rows, 0)
    loss, head_term, grad_context = decode_terms(
        context, tok_rows, mask_rows, embed, gain, w_head, add_totals
    )
    flat_term = head_term.reshape(-1)
    partial_grad = lax.psum_scatter(
        flat_term.astype(jnp.bfloat16), "dp", scatter_dimension=0, tiled=True
    ).astype(jnp.float32)
    grad_head = lax.psum_scatter(partial_grad, ("tensor", "seq"), scatter_dimension=0, tiled=True)
    product = lax.dot_general(
        lax.all_gather(grad_context, "tensor", axis=0, tiled=True),
        w_in,
        (((1,), (1,)), ((), ())),
        preferred_element_type=jnp.float32,
    )
    grad_hidden = product.astype(jnp.bfloat16)
    return (loss, grad_head, grad_hidden)


def kernel(
    sizes, hidden_h, w_in_h, embed_h, gain_h, w_head_h, tokens_h, mask_h,
    loss_o, head_o, gh_o,
    hidden, w_in, embed, gain, w_head, tokens, mask,
    ctx_own, ctx_send, ctx_recv, cnt, cnt_recv, gath, scaled, gl, hs, r1, s1, r2, s2, r3,
    gc, gh, ls1, ls1_r, ls2, ls2_r, ls3, ls3_r,
    in_sem, out_sem, ctx_ss, ctx_rs, cnt_ss, cnt_rs, gc_ss, gc_rs,
    h1_ss, h1_rs, h2_ss, h2_rs, h3_ss, h3_rs, l_ss, l_rs,
):
    DP, T, S = sizes
    a, t, s = lax.axis_index("dp"), lax.axis_index("tensor"), lax.axis_index("seq")
    steps, nframes = tokens.shape
    frames = nframes // T
    width, vocab = w_head.shape
    rows = frames * steps
    piece = width // (DP * T * S)

    barrier = pltpu.get_barrier_semaphore()
    peers_t = [{"tensor": lax.rem(t + d, T)} for d in range(1, T)]
    peers_g = [
        {"dp": lax.rem(a + d, DP), "seq": lax.rem(s + e, S)}
        for d in range(DP)
        for e in range(S)
        if d or e
    ]
    for peer in peers_t + peers_g:
        pl.semaphore_signal(barrier, inc=1, device_id=peer, device_id_type=MESH)

    loads = [
        pltpu.make_async_copy(src, dst, in_sem.at[i])
        for i, (src, dst) in enumerate(
            [
                (hidden_h, hidden),
                (w_in_h, w_in),
                (mask_h, mask),
                (tokens_h, tokens),
                (embed_h, embed),
                (gain_h, gain),
                (w_head_h, w_head),
            ]
        )
    ]
    for load in loads:
        load.start()

    sends = []

    def send(src, dst, ss, rs, peer):
        copy = pltpu.make_async_remote_copy(
            src_ref=src, dst_ref=dst, send_sem=ss, recv_sem=rs, device_id=peer, device_id_type=MESH
        )
        copy.start()
        sends.append(copy)
        return copy

    loads[0].wait()
    loads[1].wait()
    part = jnp.dot(hidden[...], w_in[...], preferred_element_type=F32).reshape(T, frames, width)
    ctx_send[...] = part.astype(BF16)
    ctx_own[...] = part
    loads[2].wait()
    mask_row = mask[...].astype(F32)
    cnt[...] = jnp.zeros(cnt.shape, F32) + jnp.sum(mask_row)
    pl.semaphore_wait(barrier, len(peers_t) + len(peers_g))
    ctx_copies = [
        send(ctx_send.at[lax.rem(t + d, T)], ctx_recv.at[d - 1], ctx_ss.at[d - 1], ctx_rs.at[d - 1],
             peers_t[d - 1])
        for d in range(1, T)
    ]
    cnt_copies = [
        send(cnt, cnt_recv.at[i], cnt_ss.at[i], cnt_rs.at[i], peer) for i, peer in enumerate(peers_g)
    ]

    loads[3].wait()
    spot = lax.broadcasted_iota(jnp.int32, (frames, nframes), 0) + t * frames
    here = lax.broadcasted_iota(jnp.int32, (frames, nframes), 1)
    mine = spot == here
    tok = tokens[...].astype(F32)
    lanes = lax.broadcasted_iota(jnp.int32, (frames, vocab), 1).astype(F32)
    hot = [
        jnp.sum(jnp.where(mine, tok[k : k + 1, :], 0.0), 1, keepdims=True) == lanes
        for k in range(steps)
    ]
    loads[4].wait()
    prev = jnp.concatenate([jnp.where(h, 1.0, 0.0).astype(BF16) for h in hot[:-1]], 0)
    gath[...] = jnp.dot(prev, embed[...], preferred_element_type=F32)
    mcol = jnp.sum(jnp.where(mine, mask_row, 0.0), 1, keepdims=True)
    loads[5].wait()
    loads[6].wait()
    gvec = gain[...]

    ctx = ctx_own[t]
    for d in range(1, T):
        ctx_copies[d - 1].wait_recv()
        ctx = ctx + ctx_recv[d - 1].astype(F32)
    ctx = ctx.astype(BF16).astype(F32)
    inputs = jnp.concatenate([ctx] * steps, 0) + jnp.concatenate(
        [jnp.zeros((frames, width), F32), gath[...]], 0
    )
    inverse = lax.rsqrt(jnp.mean(inputs * inputs, -1, keepdims=True) + 1e-06)
    normed = inputs * inverse
    flat = (normed * gvec).astype(BF16)
    scaled[...] = flat
    logits = jnp.dot(flat, w_head[...], preferred_element_type=F32)
    top = jnp.max(logits, -1, keepdims=True)
    powers = jnp.exp(logits - top)
    norm = jnp.sum(powers, -1, keepdims=True)
    total = top + jnp.log(norm)
    onehot = jnp.concatenate([jnp.where(h, 1.0, 0.0) for h in hot], 0)
    weights = jnp.concatenate([mcol] * steps, 0)
    nll = total - jnp.sum(logits * onehot, -1, keepdims=True)
    grads = ((powers * (1.0 / norm) - onehot) * weights).astype(BF16)
    gl[...] = grads

    chunk = width // DP
    order = [lax.rem(a + 1 + j, DP) for j in range(DP)]
    h1 = []
    for j in range(DP):
        c = order[j]
        cols = scaled[:, pl.ds(pl.multiple_of(c * chunk, chunk), chunk)]
        term = lax.dot_general(
            cols, gl[...], (((0,), (0,)), ((), ())), preferred_element_type=F32
        )
        hs[j] = term.astype(BF16).reshape(T, S, piece, vocab)
        for e in range(1, S):
            h1.append(
                send(hs.at[j, :, lax.rem(s + e, S)], r1.at[j, e - 1], h1_ss.at[j, e - 1],
                     h1_rs.at[j, e - 1], {"seq": lax.rem(s + e, S)})
            )
    ls1[...] = jnp.zeros(ls1.shape, F32) + jnp.sum(weights * nll)
    n = 0
    lc1 = []
    for e in range(1, S):
        lc1.append(send(ls1, ls1_r.at[e - 1], l_ss.at[n], l_rs.at[n], {"seq": lax.rem(s + e, S)}))
        n += 1

    grad_scaled = lax.dot_general(
        gl[...], w_head[...], (((1,), (1,)), ((), ())), preferred_element_type=F32
    )
    g = grad_scaled * gvec
    gi = inverse * (g - normed * jnp.mean(g * normed, -1, keepdims=True))
    gsum = gi[0:frames]
    for k in range(1, steps):
        gsum = gsum + gi[k * frames : (k + 1) * frames]
    gc[t] = gsum.astype(BF16)
    gc_copies = [
        send(gc.at[t], gc.at[t], gc_ss.at[d - 1], gc_rs.at[d - 1], peers_t[d - 1])
        for d in range(1, T)
    ]

    h2 = []
    for j in range(DP):
        acc = hs[j, :, s].astype(F32)
        for e in range(1, S):
            h1[j * (S - 1) + e - 1].wait_recv()
            acc = acc + r1[j, e - 1].astype(F32)
        s1[j] = acc.astype(BF16)
        for d in range(1, T):
            h2.append(
                send(s1.at[j, lax.rem(t + d, T)], r2.at[j, d - 1], h2_ss.at[j, d - 1],
                     h2_rs.at[j, d - 1], peers_t[d - 1])
            )
    lsum = ls1[...]
    for e in range(1, S):
        lc1[e - 1].wait_recv()
        lsum = lsum + ls1_r[e - 1]
    ls2[...] = lsum
    lc2 = []
    for d in range(1, T):
        lc2.append(send(ls2, ls2_r.at[d - 1], l_ss.at[n], l_rs.at[n], peers_t[d - 1]))
        n += 1

    total_mask = cnt[...]
    for i in range(len(peers_g)):
        cnt_copies[i].wait_recv()
        total_mask = total_mask + cnt_recv[i]
    share = 1.0 / (total_mask[0:1, 0:1] * steps)
    for d in range(1, T):
        gc_copies[d - 1].wait_recv()
    product = lax.dot_general(
        gc[...].reshape(nframes, width), w_in[...], (((1,), (1,)), ((), ())),
        preferred_element_type=F32,
    )
    gh[...] = (product * share).astype(BF16)
    out_copy = pltpu.make_async_copy(gh, gh_o, out_sem)
    out_copy.start()

    h3 = []
    for j in range(DP):
        acc = s1[j, t].astype(F32)
        for d in range(1, T):
            h2[j * (T - 1) + d - 1].wait_recv()
            acc = acc + r2[j, d - 1].astype(F32)
        if j < DP - 1:
            s2[j] = acc.astype(BF16)
            h3.append(
                send(s2.at[j], r3.at[j], h3_ss.at[j], h3_rs.at[j], {"dp": order[j]})
            )
    lsum = ls2[...]
    for d in range(1, T):
        lc2[d - 1].wait_recv()
        lsum = lsum + ls2_r[d - 1]
    ls3[...] = lsum
    lc3 = []
    for d in range(1, DP):
        lc3.append(
            send(ls3, ls3_r.at[d - 1], l_ss.at[n], l_rs.at[n], {"dp": lax.rem(a + d, DP)})
        )
        n += 1
    for j in range(DP - 1):
        h3[j].wait_recv()
        acc = acc + r3[j].astype(F32)
    acc = acc * share
    groups = vocab // 128
    for b in range(groups):
        head_o[pl.ds(b, piece, stride=groups), :] = acc[:, b * 128 : (b + 1) * 128]
    for d in range(1, DP):
        lc3[d - 1].wait_recv()
        lsum = lsum + ls3_r[d - 1]
    loss_o[...] = lsum[0:1, 0:1] * share
    out_copy.wait()
    for copy in sends:
        copy.wait_send()


def per_device_kernel(hidden, w_in, embed, gain, w_head, tokens, frame_mask):
    DP, T, S = lax.axis_size("dp"), lax.axis_size("tensor"), lax.axis_size("seq")
    nframes, feats = hidden.shape
    steps = tokens.shape[1]
    frames = nframes // T
    width, vocab = w_head.shape
    rows = frames * steps
    piece = width // (DP * T * S)
    G = DP * S - 1
    V = pltpu.VMEM
    dma = pltpu.SemaphoreType.DMA
    scratch = [
        V(hidden.shape, BF16), V(w_in.shape, BF16), V(embed.shape, BF16), V((1, width), F32),
        V(w_head.shape, BF16), V((steps, nframes), jnp.int32), V((1, nframes), jnp.int32),
        V((T, frames, width), F32),
        V((T, frames, width), BF16),
        V((T - 1, frames, width), BF16),
        V((8, 128), F32),
        V((G, 8, 128), F32),
        V((rows - frames, width), F32),
        V((rows, width), BF16),
        V((rows, vocab), BF16),
        V((DP, T, S, piece, vocab), BF16),
        V((DP, S - 1, T, piece, vocab), BF16),
        V((DP, T, piece, vocab), BF16),
        V((DP, T - 1, piece, vocab), BF16),
        V((DP - 1, piece, vocab), BF16),
        V((DP - 1, piece, vocab), BF16),
        V((T, frames, width), BF16),
        V((nframes, feats), BF16),
        V((8, 128), F32), V((S - 1, 8, 128), F32),
        V((8, 128), F32), V((T - 1, 8, 128), F32),
        V((8, 128), F32), V((DP - 1, 8, 128), F32),
        dma((7,)), dma,
        dma((T - 1,)), dma((T - 1,)), dma((G,)), dma((G,)), dma((T - 1,)), dma((T - 1,)),
        dma((DP, S - 1)), dma((DP, S - 1)), dma((DP, T - 1)), dma((DP, T - 1)),
        dma((DP - 1,)), dma((DP - 1,)), dma((S + T + DP - 3,)), dma((S + T + DP - 3,)),
    ]
    loss, head, grad_hidden = pl.pallas_call(
        functools.partial(kernel, (DP, T, S)),
        out_shape=(
            jax.ShapeDtypeStruct((1, 1), F32),
            jax.ShapeDtypeStruct((piece * vocab // 128, 128), F32),
            jax.ShapeDtypeStruct((nframes, feats), BF16),
        ),
        in_specs=[pl.BlockSpec(memory_space=pl.ANY)] * 7,
        out_specs=(
            pl.BlockSpec(memory_space=pltpu.VMEM),
            pl.BlockSpec(memory_space=pltpu.VMEM),
            pl.BlockSpec(memory_space=pl.ANY),
        ),
        scratch_shapes=scratch,
        compiler_params=pltpu.CompilerParams(
            collective_id=0, has_side_effects=True, vmem_limit_bytes=63 << 20
        ),
        name="decode",
    )(hidden, w_in, embed, gain.reshape(1, -1), w_head, tokens.T, frame_mask.reshape(1, -1))
    return loss.reshape(()), head.reshape(-1), grad_hidden


def solution(mesh):
    def per_device(hidden, w_in, embed, gain, w_head, tokens, frame_mask):
        DP, T, S = mesh.shape["dp"], mesh.shape["tensor"], mesh.shape["seq"]
        width, vocab = w_head.shape
        fits = (
            width % (16 * DP * T * S) == 0
            and width % (128 * DP) == 0
            and vocab % 128 == 0
            and hidden.shape[0] % (16 * T) == 0
            and min(DP, T, S) > 1
        )
        run = per_device_kernel if fits else per_device_plain
        return run(hidden, w_in, embed, gain, w_head, tokens, frame_mask)

    placed = (
        P(("dp", "seq"), "tensor"),
        P("tensor", None),
        P(),
        P(),
        P(),
        P(("dp", "seq"), None),
        P(("dp", "seq")),
    )
    return jax.shard_map(
        per_device,
        mesh=mesh,
        in_specs=placed,
        out_specs=(P(), P(("dp", "tensor", "seq")), P(("dp", "seq"), "tensor")),
        check_vma=False,
    )
```

```python
import functools

import jax
import jax.numpy as jnp
from jax import lax
from jax.experimental import pallas as pl
from jax.experimental.pallas import tpu as pltpu
from jax.sharding import PartitionSpec as P

F32 = jnp.float32
BF16 = jnp.bfloat16
MESH = pl.DeviceIdType.MESH


def decode_terms(context, tok_rows, mask_rows, embed, gain, w_head, count_fn):
    frames = context.shape[0]
    width = context.shape[1]
    steps = tok_rows.shape[1]
    before = embed[tok_rows[:, :-1]].astype(jnp.float32)
    leading = jnp.zeros((frames, 1, width), jnp.float32)
    inputs = context.astype(jnp.float32)[:, None, :] + jnp.concatenate([leading, before], 1)
    inverse = lax.rsqrt(jnp.mean(inputs * inputs, -1, keepdims=True) + 1e-06)
    normed = inputs * inverse
    scaled = (normed * gain).astype(jnp.bfloat16)
    flat = scaled.reshape(frames * steps, width)
    logits = jnp.dot(flat, w_head, preferred_element_type=jnp.float32)
    top = jnp.max(logits, -1, keepdims=True)
    total = top[:, 0] + jnp.log(jnp.sum(jnp.exp(logits - top), -1))
    target = tok_rows.reshape(-1)
    onehot = (target[:, None] == jnp.arange(w_head.shape[1], dtype=jnp.int32)[None, :]).astype(
        jnp.float32
    )
    nll = total - jnp.sum(logits * onehot, -1)
    weights = (mask_rows.astype(jnp.float32)[:, None] * jnp.ones((1, steps), jnp.float32)).reshape(
        -1
    )
    count, loss_sum = count_fn(
        steps * jnp.sum(mask_rows.astype(jnp.float32)), jnp.sum(weights * nll)
    )
    probs = jnp.exp(logits - total[:, None])
    grad_logits = ((probs - onehot) * weights[:, None] / count).astype(jnp.bfloat16)
    head_term = lax.dot_general(
        flat, grad_logits, (((0,), (0,)), ((), ())), preferred_element_type=jnp.float32
    )
    grad_scaled = lax.dot_general(
        grad_logits, w_head, (((1,), (1,)), ((), ())), preferred_element_type=jnp.float32
    )
    scaled_grad = grad_scaled.reshape(inputs.shape) * gain
    grad_inputs = inverse * (
        scaled_grad - normed * jnp.mean(scaled_grad * normed, -1, keepdims=True)
    )
    grad_context = jnp.sum(grad_inputs, 1).astype(jnp.bfloat16)
    return (loss_sum / count, head_term, grad_context)


def add_totals(count_local, loss_local):
    return lax.psum((count_local, loss_local), ("dp", "tensor", "seq"))


def per_device_plain(hidden, w_in, embed, gain, w_head, tokens, frame_mask):
    groups = lax.axis_size("tensor")
    rows = hidden.shape[0] // groups
    context = lax.psum_scatter(
        jnp.dot(hidden, w_in, preferred_element_type=jnp.float32),
        "tensor",
        scatter_dimension=0,
        tiled=True,
    ).astype(jnp.bfloat16)
    offset = lax.axis_index("tensor") * rows
    tok_rows = lax.dynamic_slice_in_dim(tokens, offset, rows, 0)
    mask_rows = lax.dynamic_slice_in_dim(frame_mask, offset, rows, 0)
    loss, head_term, grad_context = decode_terms(
        context, tok_rows, mask_rows, embed, gain, w_head, add_totals
    )
    flat_term = head_term.reshape(-1)
    partial_grad = lax.psum_scatter(
        flat_term.astype(jnp.bfloat16), "dp", scatter_dimension=0, tiled=True
    ).astype(jnp.float32)
    grad_head = lax.psum_scatter(partial_grad, ("tensor", "seq"), scatter_dimension=0, tiled=True)
    product = lax.dot_general(
        lax.all_gather(grad_context, "tensor", axis=0, tiled=True),
        w_in,
        (((1,), (1,)), ((), ())),
        preferred_element_type=jnp.float32,
    )
    grad_hidden = product.astype(jnp.bfloat16)
    return (loss, grad_head, grad_hidden)


def kernel(
    sizes, hidden_h, w_in_h, embed_h, gain_h, w_head_h, tokens_h, mask_h,
    loss_o, head_o, gh_o,
    hidden, w_in, embed, gain, w_head, tokens, mask,
    ctx_own, ctx_send, ctx_recv, cnt, cnt_recv, gath, scaled, gl, hs, r1, s1, r2, s2, r3,
    gc, ls1, ls1_r, ls2, ls2_r, ls3, ls3_r,
    in_sem, ctx_ss, ctx_rs, cnt_ss, cnt_rs, gc_ss, gc_rs,
    h1_ss, h1_rs, h2_ss, h2_rs, h3_ss, h3_rs, l_ss, l_rs,
):
    DP, T, S = sizes
    a, t, s = lax.axis_index("dp"), lax.axis_index("tensor"), lax.axis_index("seq")
    steps, nframes = tokens.shape
    frames = nframes // T
    width, vocab = w_head.shape
    rows = frames * steps
    piece = width // (DP * T * S)

    barrier = pltpu.get_barrier_semaphore()
    peers_t = [{"tensor": lax.rem(t + d, T)} for d in range(1, T)]
    peers_g = [
        {"dp": lax.rem(a + d, DP), "seq": lax.rem(s + e, S)}
        for d in range(DP)
        for e in range(S)
        if d or e
    ]
    for peer in peers_t + peers_g:
        pl.semaphore_signal(barrier, inc=1, device_id=peer, device_id_type=MESH)

    loads = [
        pltpu.make_async_copy(src, dst, in_sem.at[i])
        for i, (src, dst) in enumerate(
            [
                (hidden_h, hidden),
                (w_in_h, w_in),
                (mask_h, mask),
                (tokens_h, tokens),
                (embed_h, embed),
                (gain_h, gain),
                (w_head_h, w_head),
            ]
        )
    ]
    for load in loads:
        load.start()

    sends, seen = [], set()

    def got(copy):
        copy.wait_recv()
        seen.add(id(copy))

    def send(src, dst, ss, rs, peer):
        copy = pltpu.make_async_remote_copy(
            src_ref=src, dst_ref=dst, send_sem=ss, recv_sem=rs, device_id=peer, device_id_type=MESH
        )
        copy.start()
        sends.append(copy)
        return copy

    loads[0].wait()
    loads[1].wait()
    part = jnp.dot(hidden[...], w_in[...], preferred_element_type=F32).reshape(T, frames, width)
    ctx_send[...] = part.astype(BF16)
    ctx_own[...] = part
    loads[2].wait()
    mask_row = mask[...].astype(F32)
    cnt[...] = jnp.zeros(cnt.shape, F32) + jnp.sum(mask_row)
    pl.semaphore_wait(barrier, len(peers_t) + len(peers_g))
    ctx_copies = [
        send(ctx_send.at[lax.rem(t + d, T)], ctx_recv.at[d - 1], ctx_ss.at[d - 1], ctx_rs.at[d - 1],
             peers_t[d - 1])
        for d in range(1, T)
    ]
    cnt_copies = [
        send(cnt, cnt_recv.at[i], cnt_ss.at[i], cnt_rs.at[i], peer) for i, peer in enumerate(peers_g)
    ]

    loads[3].wait()
    spot = lax.broadcasted_iota(jnp.int32, (frames, nframes), 0) + t * frames
    here = lax.broadcasted_iota(jnp.int32, (frames, nframes), 1)
    mine = spot == here
    tok = tokens[...].astype(F32)
    lanes = lax.broadcasted_iota(jnp.int32, (frames, vocab), 1).astype(F32)
    hot = [
        jnp.sum(jnp.where(mine, tok[k : k + 1, :], 0.0), 1, keepdims=True) == lanes
        for k in range(steps)
    ]
    loads[4].wait()
    prev = jnp.concatenate([jnp.where(h, 1.0, 0.0).astype(BF16) for h in hot[:-1]], 0)
    gath[...] = jnp.dot(prev, embed[...], preferred_element_type=F32)
    mcol = jnp.sum(jnp.where(mine, mask_row, 0.0), 1, keepdims=True)
    loads[5].wait()
    loads[6].wait()
    gvec = gain[...]

    ctx = ctx_own[t]
    for d in range(1, T):
        got(ctx_copies[d - 1])
        ctx = ctx + ctx_recv[d - 1].astype(F32)
    ctx = ctx.astype(BF16).astype(F32)
    inputs = jnp.concatenate([ctx] * steps, 0) + jnp.concatenate(
        [jnp.zeros((frames, width), F32), gath[...]], 0
    )
    inverse = lax.rsqrt(jnp.mean(inputs * inputs, -1, keepdims=True) + 1e-06)
    normed = inputs * inverse
    flat = (normed * gvec).astype(BF16)
    scaled[...] = flat
    logits = jnp.dot(flat, w_head[...], preferred_element_type=F32)
    top = jnp.max(logits, -1, keepdims=True)
    powers = jnp.exp(logits - top)
    norm = jnp.sum(powers, -1, keepdims=True)
    total = top + jnp.log(norm)
    onehot = jnp.concatenate([jnp.where(h, 1.0, 0.0) for h in hot], 0)
    weights = jnp.concatenate([mcol] * steps, 0)
    nll = total - jnp.sum(logits * onehot, -1, keepdims=True)
    grads = ((powers * (1.0 / norm) - onehot) * weights).astype(BF16)
    gl[...] = grads

    chunk = width // DP
    order = [lax.rem(a + 1 + j, DP) for j in range(DP)]
    h1 = []
    for j in range(DP):
        c = order[j]
        cols = scaled[:, pl.ds(pl.multiple_of(c * chunk, chunk), chunk)]
        term = lax.dot_general(
            cols, gl[...], (((0,), (0,)), ((), ())), preferred_element_type=F32
        )
        hs[j] = term.astype(BF16).reshape(T, S, piece, vocab)
        for e in range(1, S):
            h1.append(
                send(hs.at[j, :, lax.rem(s + e, S)], r1.at[j, e - 1], h1_ss.at[j, e - 1],
                     h1_rs.at[j, e - 1], {"seq": lax.rem(s + e, S)})
            )
    ls1[...] = jnp.zeros(ls1.shape, F32) + jnp.sum(weights * nll)
    n = 0
    lc1 = []
    for e in range(1, S):
        lc1.append(send(ls1, ls1_r.at[e - 1], l_ss.at[n], l_rs.at[n], {"seq": lax.rem(s + e, S)}))
        n += 1

    grad_scaled = lax.dot_general(
        gl[...], w_head[...], (((1,), (1,)), ((), ())), preferred_element_type=F32
    )
    g = grad_scaled * gvec
    gi = inverse * (g - normed * jnp.mean(g * normed, -1, keepdims=True))
    gsum = gi[0:frames]
    for k in range(1, steps):
        gsum = gsum + gi[k * frames : (k + 1) * frames]
    gc[t] = gsum.astype(BF16)
    gc_copies = [
        send(gc.at[t], gc.at[t], gc_ss.at[d - 1], gc_rs.at[d - 1], peers_t[d - 1])
        for d in range(1, T)
    ]

    h2 = []
    for j in range(DP):
        acc = hs[j, :, s].astype(F32)
        for e in range(1, S):
            got(h1[j * (S - 1) + e - 1])
            acc = acc + r1[j, e - 1].astype(F32)
        s1[j] = acc.astype(BF16)
        for d in range(1, T):
            h2.append(
                send(s1.at[j, lax.rem(t + d, T)], r2.at[j, d - 1], h2_ss.at[j, d - 1],
                     h2_rs.at[j, d - 1], peers_t[d - 1])
            )
    lsum = ls1[...]
    for e in range(1, S):
        got(lc1[e - 1])
        lsum = lsum + ls1_r[e - 1]
    ls2[...] = lsum
    lc2 = []
    for d in range(1, T):
        lc2.append(send(ls2, ls2_r.at[d - 1], l_ss.at[n], l_rs.at[n], peers_t[d - 1]))
        n += 1

    total_mask = cnt[...]
    for i in range(len(peers_g)):
        got(cnt_copies[i])
        total_mask = total_mask + cnt_recv[i]
    share = 1.0 / (total_mask[0:1, 0:1] * steps)
    for d in range(1, T):
        got(gc_copies[d - 1])
    product = lax.dot_general(
        gc[...].reshape(nframes, width), w_in[...], (((1,), (1,)), ((), ())),
        preferred_element_type=F32,
    )
    gh_o[...] = (product * share).astype(BF16)

    h3 = []
    for j in range(DP):
        acc = s1[j, t].astype(F32)
        for d in range(1, T):
            got(h2[j * (T - 1) + d - 1])
            acc = acc + r2[j, d - 1].astype(F32)
        if j < DP - 1:
            s2[j] = acc.astype(BF16)
            h3.append(
                send(s2.at[j], r3.at[j], h3_ss.at[j], h3_rs.at[j], {"dp": order[j]})
            )
    lsum = ls2[...]
    for d in range(1, T):
        got(lc2[d - 1])
        lsum = lsum + ls2_r[d - 1]
    ls3[...] = lsum
    lc3 = []
    for d in range(1, DP):
        lc3.append(
            send(ls3, ls3_r.at[d - 1], l_ss.at[n], l_rs.at[n], {"dp": lax.rem(a + d, DP)})
        )
        n += 1
    for j in range(DP - 1):
        got(h3[j])
        acc = acc + r3[j].astype(F32)
    acc = acc * share
    groups = vocab // 128
    for b in range(groups):
        head_o[pl.ds(b, piece, stride=groups), :] = acc[:, b * 128 : (b + 1) * 128]
    for d in range(1, DP):
        got(lc3[d - 1])
        lsum = lsum + ls3_r[d - 1]
    loss_o[...] = lsum[0:1, 0:1] * share
    for copy in sends:
        copy.wait_send()


def write_out(loss_i, head_i, gh_i, loss_o, head_o, gh_o, sem):
    copies = [
        pltpu.make_async_copy(src, dst, sem.at[i])
        for i, (src, dst) in enumerate([(gh_i, gh_o), (head_i, head_o), (loss_i, loss_o)])
    ]
    for copy in copies:
        copy.start()
    for copy in copies:
        copy.wait()


def per_device_kernel(hidden, w_in, embed, gain, w_head, tokens, frame_mask):
    DP, T, S = lax.axis_size("dp"), lax.axis_size("tensor"), lax.axis_size("seq")
    nframes, feats = hidden.shape
    steps = tokens.shape[1]
    frames = nframes // T
    width, vocab = w_head.shape
    rows = frames * steps
    piece = width // (DP * T * S)
    G = DP * S - 1
    V = pltpu.VMEM
    dma = pltpu.SemaphoreType.DMA
    scratch = [
        V(hidden.shape, BF16), V(w_in.shape, BF16), V(embed.shape, BF16), V((1, width), F32),
        V(w_head.shape, BF16), V((steps, nframes), jnp.int32), V((1, nframes), jnp.int32),
        V((T, frames, width), F32),
        V((T, frames, width), BF16),
        V((T - 1, frames, width), BF16),
        V((8, 128), F32),
        V((G, 8, 128), F32),
        V((rows - frames, width), F32),
        V((rows, width), BF16),
        V((rows, vocab), BF16),
        V((DP, T, S, piece, vocab), BF16),
        V((DP, S - 1, T, piece, vocab), BF16),
        V((DP, T, piece, vocab), BF16),
        V((DP, T - 1, piece, vocab), BF16),
        V((DP - 1, piece, vocab), BF16),
        V((DP - 1, piece, vocab), BF16),
        V((T, frames, width), BF16),
        V((8, 128), F32), V((S - 1, 8, 128), F32),
        V((8, 128), F32), V((T - 1, 8, 128), F32),
        V((8, 128), F32), V((DP - 1, 8, 128), F32),
        dma((7,)),
        dma((T - 1,)), dma((T - 1,)), dma((G,)), dma((G,)), dma((T - 1,)), dma((T - 1,)),
        dma((DP, S - 1)), dma((DP, S - 1)), dma((DP, T - 1)), dma((DP, T - 1)),
        dma((DP - 1,)), dma((DP - 1,)), dma((S + T + DP - 3,)), dma((S + T + DP - 3,)),
    ]
    shapes = (
        jax.ShapeDtypeStruct((1, 1), F32),
        jax.ShapeDtypeStruct((piece * vocab // 128, 128), F32),
        jax.ShapeDtypeStruct((nframes, feats), BF16),
    )
    vmem = pl.BlockSpec(memory_space=pltpu.VMEM)
    results = pl.pallas_call(
        functools.partial(kernel, (DP, T, S)),
        out_shape=shapes,
        in_specs=[pl.BlockSpec(memory_space=pltpu.HBM)] * 7,
        out_specs=(vmem, vmem, vmem),
        scratch_shapes=scratch,
        compiler_params=pltpu.CompilerParams(
            collective_id=0, has_side_effects=True, vmem_limit_bytes=40 << 20
        ),
        name="decode",
    )(*[pltpu.with_memory_space_constraint(x, pltpu.HBM) for x in (hidden, w_in, embed, gain.reshape(1, -1), w_head, tokens.T, frame_mask.reshape(1, -1))])
    loss, head, grad_hidden = pl.pallas_call(
        write_out,
        out_shape=shapes,
        in_specs=[pl.BlockSpec(memory_space=pl.ANY)] * 3,
        out_specs=(pl.BlockSpec(memory_space=pltpu.HBM),) * 3,
        scratch_shapes=[dma((3,))],
        compiler_params=pltpu.CompilerParams(vmem_limit_bytes=4 << 20),
        name="write_out",
    )(*results)
    return loss.reshape(()), head.reshape(-1), grad_hidden


def solution(mesh):
    def per_device(hidden, w_in, embed, gain, w_head, tokens, frame_mask):
        DP, T, S = mesh.shape["dp"], mesh.shape["tensor"], mesh.shape["seq"]
        width, vocab = w_head.shape
        fits = (
            width % (16 * DP * T * S) == 0
            and width % (128 * DP) == 0
            and vocab % 128 == 0
            and hidden.shape[0] % (16 * T) == 0
            and min(DP, T, S) > 1
        )
        run = per_device_kernel if fits else per_device_plain
        return run(hidden, w_in, embed, gain, w_head, tokens, frame_mask)

    placed = (
        P(("dp", "seq"), "tensor"),
        P("tensor", None),
        P(),
        P(),
        P(),
        P(("dp", "seq"), None),
        P(("dp", "seq")),
    )
    return jax.shard_map(
        per_device,
        mesh=mesh,
        in_specs=placed,
        out_specs=(P(), P(("dp", "tensor", "seq")), P(("dp", "seq"), "tensor")),
        check_vma=False,
    )
```

```python
import functools

import jax
import jax.numpy as jnp
from jax import lax
from jax.experimental import pallas as pl
from jax.experimental.pallas import tpu as pltpu
from jax.sharding import PartitionSpec as P

F32 = jnp.float32
BF16 = jnp.bfloat16
MESH = pl.DeviceIdType.MESH


def decode_terms(context, tok_rows, mask_rows, embed, gain, w_head, count_fn):
    frames = context.shape[0]
    width = context.shape[1]
    steps = tok_rows.shape[1]
    before = embed[tok_rows[:, :-1]].astype(jnp.float32)
    leading = jnp.zeros((frames, 1, width), jnp.float32)
    inputs = context.astype(jnp.float32)[:, None, :] + jnp.concatenate([leading, before], 1)
    inverse = lax.rsqrt(jnp.mean(inputs * inputs, -1, keepdims=True) + 1e-06)
    normed = inputs * inverse
    scaled = (normed * gain).astype(jnp.bfloat16)
    flat = scaled.reshape(frames * steps, width)
    logits = jnp.dot(flat, w_head, preferred_element_type=jnp.float32)
    top = jnp.max(logits, -1, keepdims=True)
    total = top[:, 0] + jnp.log(jnp.sum(jnp.exp(logits - top), -1))
    target = tok_rows.reshape(-1)
    onehot = (target[:, None] == jnp.arange(w_head.shape[1], dtype=jnp.int32)[None, :]).astype(
        jnp.float32
    )
    nll = total - jnp.sum(logits * onehot, -1)
    weights = (mask_rows.astype(jnp.float32)[:, None] * jnp.ones((1, steps), jnp.float32)).reshape(
        -1
    )
    count, loss_sum = count_fn(
        steps * jnp.sum(mask_rows.astype(jnp.float32)), jnp.sum(weights * nll)
    )
    probs = jnp.exp(logits - total[:, None])
    grad_logits = ((probs - onehot) * weights[:, None] / count).astype(jnp.bfloat16)
    head_term = lax.dot_general(
        flat, grad_logits, (((0,), (0,)), ((), ())), preferred_element_type=jnp.float32
    )
    grad_scaled = lax.dot_general(
        grad_logits, w_head, (((1,), (1,)), ((), ())), preferred_element_type=jnp.float32
    )
    scaled_grad = grad_scaled.reshape(inputs.shape) * gain
    grad_inputs = inverse * (
        scaled_grad - normed * jnp.mean(scaled_grad * normed, -1, keepdims=True)
    )
    grad_context = jnp.sum(grad_inputs, 1).astype(jnp.bfloat16)
    return (loss_sum / count, head_term, grad_context)


def add_totals(count_local, loss_local):
    return lax.psum((count_local, loss_local), ("dp", "tensor", "seq"))


def per_device_plain(hidden, w_in, embed, gain, w_head, tokens, frame_mask):
    groups = lax.axis_size("tensor")
    rows = hidden.shape[0] // groups
    context = lax.psum_scatter(
        jnp.dot(hidden, w_in, preferred_element_type=jnp.float32),
        "tensor",
        scatter_dimension=0,
        tiled=True,
    ).astype(jnp.bfloat16)
    offset = lax.axis_index("tensor") * rows
    tok_rows = lax.dynamic_slice_in_dim(tokens, offset, rows, 0)
    mask_rows = lax.dynamic_slice_in_dim(frame_mask, offset, rows, 0)
    loss, head_term, grad_context = decode_terms(
        context, tok_rows, mask_rows, embed, gain, w_head, add_totals
    )
    flat_term = head_term.reshape(-1)
    partial_grad = lax.psum_scatter(
        flat_term.astype(jnp.bfloat16), "dp", scatter_dimension=0, tiled=True
    ).astype(jnp.float32)
    grad_head = lax.psum_scatter(partial_grad, ("tensor", "seq"), scatter_dimension=0, tiled=True)
    product = lax.dot_general(
        lax.all_gather(grad_context, "tensor", axis=0, tiled=True),
        w_in,
        (((1,), (1,)), ((), ())),
        preferred_element_type=jnp.float32,
    )
    grad_hidden = product.astype(jnp.bfloat16)
    return (loss, grad_head, grad_hidden)


def kernel(
    sizes, hidden_h, w_in_h, embed_h, gain_h, w_head_h, tokens_h, mask_h,
    loss_o, head_o, gh_o,
    hidden, w_in, embed, gain, w_head, tokens, mask,
    ctx_own, ctx_send, ctx_recv, cnt, cnt_recv, gath, scaled, gl, hs, r1, s1, r2, s2, r3,
    gc, ls1, ls1_r, ls2, ls2_r, ls3, ls3_r,
    in_sem, ctx_ss, ctx_rs, cnt_ss, cnt_rs, gc_ss, gc_rs,
    h1_ss, h1_rs, h2_ss, h2_rs, h3_ss, h3_rs, l_ss, l_rs,
):
    DP, T, S = sizes
    a, t, s = lax.axis_index("dp"), lax.axis_index("tensor"), lax.axis_index("seq")
    steps, nframes = tokens.shape
    frames = nframes // T
    width, vocab = w_head.shape
    rows = frames * steps
    piece = width // (DP * T * S)

    barrier = pltpu.get_barrier_semaphore()
    peers_t = [{"tensor": lax.rem(t + d, T)} for d in range(1, T)]
    peers_g = [
        {"dp": lax.rem(a + d, DP), "seq": lax.rem(s + e, S)}
        for d in range(DP)
        for e in range(S)
        if d or e
    ]
    for peer in peers_t + peers_g:
        pl.semaphore_signal(barrier, inc=1, device_id=peer, device_id_type=MESH)

    loads = [
        pltpu.make_async_copy(src, dst, in_sem.at[i])
        for i, (src, dst) in enumerate(
            [
                (hidden_h, hidden),
                (w_in_h, w_in),
                (mask_h, mask),
                (tokens_h, tokens),
                (embed_h, embed),
                (gain_h, gain),
                (w_head_h, w_head),
            ]
        )
    ]
    for load in loads:
        load.start()

    sends, seen = [], set()

    def got(copy):
        copy.wait_recv()
        seen.add(id(copy))

    def send(src, dst, ss, rs, peer):
        copy = pltpu.make_async_remote_copy(
            src_ref=src, dst_ref=dst, send_sem=ss, recv_sem=rs, device_id=peer, device_id_type=MESH
        )
        copy.start()
        sends.append(copy)
        return copy

    loads[0].wait()
    loads[1].wait()
    part = jnp.dot(hidden[...], w_in[...], preferred_element_type=F32).reshape(T, frames, width)
    ctx_send[...] = part.astype(BF16)
    ctx_own[...] = part
    loads[2].wait()
    mask_row = mask[...].astype(F32)
    cnt[...] = jnp.zeros(cnt.shape, F32) + jnp.sum(mask_row)
    pl.semaphore_wait(barrier, len(peers_t) + len(peers_g))
    ctx_copies = [
        send(ctx_send.at[lax.rem(t + d, T)], ctx_recv.at[d - 1], ctx_ss.at[d - 1], ctx_rs.at[d - 1],
             peers_t[d - 1])
        for d in range(1, T)
    ]
    cnt_copies = [
        send(cnt, cnt_recv.at[i], cnt_ss.at[i], cnt_rs.at[i], peer) for i, peer in enumerate(peers_g)
    ]

    loads[3].wait()
    spot = lax.broadcasted_iota(jnp.int32, (frames, nframes), 0) + t * frames
    here = lax.broadcasted_iota(jnp.int32, (frames, nframes), 1)
    mine = spot == here
    tok = tokens[...].astype(F32)
    lanes = lax.broadcasted_iota(jnp.int32, (frames, vocab), 1).astype(F32)
    hot = [
        jnp.sum(jnp.where(mine, tok[k : k + 1, :], 0.0), 1, keepdims=True) == lanes
        for k in range(steps)
    ]
    loads[4].wait()
    prev = jnp.concatenate([jnp.where(h, 1.0, 0.0).astype(BF16) for h in hot[:-1]], 0)
    gath[...] = jnp.dot(prev, embed[...], preferred_element_type=F32)
    mcol = jnp.sum(jnp.where(mine, mask_row, 0.0), 1, keepdims=True)
    loads[5].wait()
    loads[6].wait()
    gvec = gain[...]

    ctx = ctx_own[t]
    for d in range(1, T):
        got(ctx_copies[d - 1])
        ctx = ctx + ctx_recv[d - 1].astype(F32)
    ctx = ctx.astype(BF16).astype(F32)
    inputs = jnp.concatenate([ctx] * steps, 0) + jnp.concatenate(
        [jnp.zeros((frames, width), F32), gath[...]], 0
    )
    inverse = lax.rsqrt(jnp.mean(inputs * inputs, -1, keepdims=True) + 1e-06)
    normed = inputs * inverse
    flat = (normed * gvec).astype(BF16)
    scaled[...] = flat
    logits = jnp.dot(flat, w_head[...], preferred_element_type=F32)
    top = jnp.max(logits, -1, keepdims=True)
    powers = jnp.exp(logits - top)
    norm = jnp.sum(powers, -1, keepdims=True)
    total = top + jnp.log(norm)
    onehot = jnp.concatenate([jnp.where(h, 1.0, 0.0) for h in hot], 0)
    weights = jnp.concatenate([mcol] * steps, 0)
    nll = total - jnp.sum(logits * onehot, -1, keepdims=True)
    grads = ((powers * (1.0 / norm) - onehot) * weights).astype(BF16)
    gl[...] = grads

    chunk = width // DP
    order = []
    for j in range(DP - 1):
        up = jnp.where(j < a, j, j + 1)
        down = jnp.where(DP - 1 - j > a, DP - 1 - j, DP - 2 - j)
        order.append(jnp.where(2 * a < DP, down, up))
    order.append(a)
    h1 = []
    for j in range(DP):
        c = order[j]
        cols = scaled[:, pl.ds(pl.multiple_of(c * chunk, chunk), chunk)]
        term = lax.dot_general(
            cols, gl[...], (((0,), (0,)), ((), ())), preferred_element_type=F32
        )
        hs[j] = term.astype(BF16).reshape(T, S, piece, vocab)
        for e in range(1, S):
            h1.append(
                send(hs.at[j, :, lax.rem(s + e, S)], r1.at[j, e - 1], h1_ss.at[j, e - 1],
                     h1_rs.at[j, e - 1], {"seq": lax.rem(s + e, S)})
            )
    ls1[...] = jnp.zeros(ls1.shape, F32) + jnp.sum(weights * nll)
    n = 0
    lc1 = []
    for e in range(1, S):
        lc1.append(send(ls1, ls1_r.at[e - 1], l_ss.at[n], l_rs.at[n], {"seq": lax.rem(s + e, S)}))
        n += 1

    h2 = []
    for j in range(DP):
        acc = hs[j, :, s].astype(F32)
        for e in range(1, S):
            got(h1[j * (S - 1) + e - 1])
            acc = acc + r1[j, e - 1].astype(F32)
        s1[j] = acc.astype(BF16)
        for d in range(1, T):
            h2.append(
                send(s1.at[j, lax.rem(t + d, T)], r2.at[j, d - 1], h2_ss.at[j, d - 1],
                     h2_rs.at[j, d - 1], peers_t[d - 1])
            )
    lsum = ls1[...]
    for e in range(1, S):
        got(lc1[e - 1])
        lsum = lsum + ls1_r[e - 1]
    ls2[...] = lsum
    lc2 = []
    for d in range(1, T):
        lc2.append(send(ls2, ls2_r.at[d - 1], l_ss.at[n], l_rs.at[n], peers_t[d - 1]))
        n += 1

    grad_scaled = lax.dot_general(
        gl[...], w_head[...], (((1,), (1,)), ((), ())), preferred_element_type=F32
    )
    g = grad_scaled * gvec
    gi = inverse * (g - normed * jnp.mean(g * normed, -1, keepdims=True))
    gsum = gi[0:frames]
    for k in range(1, steps):
        gsum = gsum + gi[k * frames : (k + 1) * frames]
    gc[t] = gsum.astype(BF16)
    gc_copies = [
        send(gc.at[t], gc.at[t], gc_ss.at[d - 1], gc_rs.at[d - 1], peers_t[d - 1])
        for d in range(1, T)
    ]

    total_mask = cnt[...]
    for i in range(len(peers_g)):
        got(cnt_copies[i])
        total_mask = total_mask + cnt_recv[i]
    share = 1.0 / (total_mask[0:1, 0:1] * steps)
    for d in range(1, T):
        got(gc_copies[d - 1])
    product = lax.dot_general(
        gc[...].reshape(nframes, width), w_in[...], (((1,), (1,)), ((), ())),
        preferred_element_type=F32,
    )
    gh_o[...] = (product * share).astype(BF16)

    h3 = []
    for j in range(DP):
        acc = s1[j, t].astype(F32)
        for d in range(1, T):
            got(h2[j * (T - 1) + d - 1])
            acc = acc + r2[j, d - 1].astype(F32)
        if j < DP - 1:
            s2[j] = acc.astype(BF16)
            slot = lax.rem(order[j] - a + DP, DP) - 1
            h3.append(
                send(s2.at[j], r3.at[slot], h3_ss.at[j], h3_rs.at[slot], {"dp": order[j]})
            )
    lsum = ls2[...]
    for d in range(1, T):
        got(lc2[d - 1])
        lsum = lsum + ls2_r[d - 1]
    ls3[...] = lsum
    lc3 = []
    for d in range(1, DP):
        lc3.append(
            send(ls3, ls3_r.at[d - 1], l_ss.at[n], l_rs.at[n], {"dp": lax.rem(a + d, DP)})
        )
        n += 1
    for j in range(DP - 1):
        arrival = pltpu.make_async_remote_copy(
            src_ref=s2.at[j], dst_ref=r3.at[j], send_sem=h3_ss.at[j], recv_sem=h3_rs.at[j],
            device_id={"dp": lax.rem(a + 1, DP)}, device_id_type=MESH,
        )
        arrival.wait_recv()
        acc = acc + r3[j].astype(F32)
    acc = acc * share
    groups = vocab // 128
    for b in range(groups):
        head_o[pl.ds(b, piece, stride=groups), :] = acc[:, b * 128 : (b + 1) * 128]
    for d in range(1, DP):
        got(lc3[d - 1])
        lsum = lsum + ls3_r[d - 1]
    loss_o[...] = lsum[0:1, 0:1] * share
    for copy in sends:
        copy.wait_send()


def write_out(loss_i, head_i, gh_i, loss_o, head_o, gh_o, sem):
    copies = [
        pltpu.make_async_copy(src, dst, sem.at[i])
        for i, (src, dst) in enumerate([(gh_i, gh_o), (head_i, head_o), (loss_i, loss_o)])
    ]
    for copy in copies:
        copy.start()
    for copy in copies:
        copy.wait()


def per_device_kernel(hidden, w_in, embed, gain, w_head, tokens, frame_mask):
    DP, T, S = lax.axis_size("dp"), lax.axis_size("tensor"), lax.axis_size("seq")
    nframes, feats = hidden.shape
    steps = tokens.shape[1]
    frames = nframes // T
    width, vocab = w_head.shape
    rows = frames * steps
    piece = width // (DP * T * S)
    G = DP * S - 1
    V = pltpu.VMEM
    dma = pltpu.SemaphoreType.DMA
    scratch = [
        V(hidden.shape, BF16), V(w_in.shape, BF16), V(embed.shape, BF16), V((1, width), F32),
        V(w_head.shape, BF16), V((steps, nframes), jnp.int32), V((1, nframes), jnp.int32),
        V((T, frames, width), F32),
        V((T, frames, width), BF16),
        V((T - 1, frames, width), BF16),
        V((8, 128), F32),
        V((G, 8, 128), F32),
        V((rows - frames, width), F32),
        V((rows, width), BF16),
        V((rows, vocab), BF16),
        V((DP, T, S, piece, vocab), BF16),
        V((DP, S - 1, T, piece, vocab), BF16),
        V((DP, T, piece, vocab), BF16),
        V((DP, T - 1, piece, vocab), BF16),
        V((DP - 1, piece, vocab), BF16),
        V((DP - 1, piece, vocab), BF16),
        V((T, frames, width), BF16),
        V((8, 128), F32), V((S - 1, 8, 128), F32),
        V((8, 128), F32), V((T - 1, 8, 128), F32),
        V((8, 128), F32), V((DP - 1, 8, 128), F32),
        dma((7,)),
        dma((T - 1,)), dma((T - 1,)), dma((G,)), dma((G,)), dma((T - 1,)), dma((T - 1,)),
        dma((DP, S - 1)), dma((DP, S - 1)), dma((DP, T - 1)), dma((DP, T - 1)),
        dma((DP - 1,)), dma((DP - 1,)), dma((S + T + DP - 3,)), dma((S + T + DP - 3,)),
    ]
    shapes = (
        jax.ShapeDtypeStruct((1, 1), F32),
        jax.ShapeDtypeStruct((piece * vocab // 128, 128), F32),
        jax.ShapeDtypeStruct((nframes, feats), BF16),
    )
    vmem = pl.BlockSpec(memory_space=pltpu.VMEM)
    results = pl.pallas_call(
        functools.partial(kernel, (DP, T, S)),
        out_shape=shapes,
        in_specs=[pl.BlockSpec(memory_space=pltpu.HBM)] * 7,
        out_specs=(vmem, vmem, vmem),
        scratch_shapes=scratch,
        compiler_params=pltpu.CompilerParams(
            collective_id=0, has_side_effects=True, vmem_limit_bytes=40 << 20
        ),
        name="decode",
    )(*[pltpu.with_memory_space_constraint(x, pltpu.HBM) for x in (hidden, w_in, embed, gain.reshape(1, -1), w_head, tokens.T, frame_mask.reshape(1, -1))])
    loss, head, grad_hidden = pl.pallas_call(
        write_out,
        out_shape=shapes,
        in_specs=[pl.BlockSpec(memory_space=pl.ANY)] * 3,
        out_specs=(pl.BlockSpec(memory_space=pltpu.HBM),) * 3,
        scratch_shapes=[dma((3,))],
        compiler_params=pltpu.CompilerParams(vmem_limit_bytes=4 << 20),
        name="write_out",
    )(*results)
    return loss.reshape(()), head.reshape(-1), grad_hidden


def solution(mesh):
    def per_device(hidden, w_in, embed, gain, w_head, tokens, frame_mask):
        DP, T, S = mesh.shape["dp"], mesh.shape["tensor"], mesh.shape["seq"]
        width, vocab = w_head.shape
        fits = (
            width % (16 * DP * T * S) == 0
            and width % (128 * DP) == 0
            and vocab % 128 == 0
            and hidden.shape[0] % (16 * T) == 0
            and min(DP, T, S) > 1
        )
        run = per_device_kernel if fits else per_device_plain
        return run(hidden, w_in, embed, gain, w_head, tokens, frame_mask)

    placed = (
        P(("dp", "seq"), "tensor"),
        P("tensor", None),
        P(),
        P(),
        P(),
        P(("dp", "seq"), None),
        P(("dp", "seq")),
    )
    return jax.shard_map(
        per_device,
        mesh=mesh,
        in_specs=placed,
        out_specs=(P(), P(("dp", "tensor", "seq")), P(("dp", "seq"), "tensor")),
        check_vma=False,
    )
```

```python
import functools

import jax
import jax.numpy as jnp
from jax import lax
from jax.experimental import pallas as pl
from jax.experimental.pallas import tpu as pltpu
from jax.sharding import PartitionSpec as P

F32 = jnp.float32
BF16 = jnp.bfloat16
MESH = pl.DeviceIdType.MESH


def decode_terms(context, tok_rows, mask_rows, embed, gain, w_head, count_fn):
    frames = context.shape[0]
    width = context.shape[1]
    steps = tok_rows.shape[1]
    before = embed[tok_rows[:, :-1]].astype(jnp.float32)
    leading = jnp.zeros((frames, 1, width), jnp.float32)
    inputs = context.astype(jnp.float32)[:, None, :] + jnp.concatenate([leading, before], 1)
    inverse = lax.rsqrt(jnp.mean(inputs * inputs, -1, keepdims=True) + 1e-06)
    normed = inputs * inverse
    scaled = (normed * gain).astype(jnp.bfloat16)
    flat = scaled.reshape(frames * steps, width)
    logits = jnp.dot(flat, w_head, preferred_element_type=jnp.float32)
    top = jnp.max(logits, -1, keepdims=True)
    total = top[:, 0] + jnp.log(jnp.sum(jnp.exp(logits - top), -1))
    target = tok_rows.reshape(-1)
    onehot = (target[:, None] == jnp.arange(w_head.shape[1], dtype=jnp.int32)[None, :]).astype(
        jnp.float32
    )
    nll = total - jnp.sum(logits * onehot, -1)
    weights = (mask_rows.astype(jnp.float32)[:, None] * jnp.ones((1, steps), jnp.float32)).reshape(
        -1
    )
    count, loss_sum = count_fn(
        steps * jnp.sum(mask_rows.astype(jnp.float32)), jnp.sum(weights * nll)
    )
    probs = jnp.exp(logits - total[:, None])
    grad_logits = ((probs - onehot) * weights[:, None] / count).astype(jnp.bfloat16)
    head_term = lax.dot_general(
        flat, grad_logits, (((0,), (0,)), ((), ())), preferred_element_type=jnp.float32
    )
    grad_scaled = lax.dot_general(
        grad_logits, w_head, (((1,), (1,)), ((), ())), preferred_element_type=jnp.float32
    )
    scaled_grad = grad_scaled.reshape(inputs.shape) * gain
    grad_inputs = inverse * (
        scaled_grad - normed * jnp.mean(scaled_grad * normed, -1, keepdims=True)
    )
    grad_context = jnp.sum(grad_inputs, 1).astype(jnp.bfloat16)
    return (loss_sum / count, head_term, grad_context)


def add_totals(count_local, loss_local):
    return lax.psum((count_local, loss_local), ("dp", "tensor", "seq"))


def per_device_plain(hidden, w_in, embed, gain, w_head, tokens, frame_mask):
    groups = lax.axis_size("tensor")
    rows = hidden.shape[0] // groups
    context = lax.psum_scatter(
        jnp.dot(hidden, w_in, preferred_element_type=jnp.float32),
        "tensor",
        scatter_dimension=0,
        tiled=True,
    ).astype(jnp.bfloat16)
    offset = lax.axis_index("tensor") * rows
    tok_rows = lax.dynamic_slice_in_dim(tokens, offset, rows, 0)
    mask_rows = lax.dynamic_slice_in_dim(frame_mask, offset, rows, 0)
    loss, head_term, grad_context = decode_terms(
        context, tok_rows, mask_rows, embed, gain, w_head, add_totals
    )
    flat_term = head_term.reshape(-1)
    partial_grad = lax.psum_scatter(
        flat_term.astype(jnp.bfloat16), "dp", scatter_dimension=0, tiled=True
    ).astype(jnp.float32)
    grad_head = lax.psum_scatter(partial_grad, ("tensor", "seq"), scatter_dimension=0, tiled=True)
    product = lax.dot_general(
        lax.all_gather(grad_context, "tensor", axis=0, tiled=True),
        w_in,
        (((1,), (1,)), ((), ())),
        preferred_element_type=jnp.float32,
    )
    grad_hidden = product.astype(jnp.bfloat16)
    return (loss, grad_head, grad_hidden)


def kernel(
    sizes, hidden_h, w_in_h, embed_h, gain_h, w_head_h, tokens_h, mask_h,
    loss_o, head_o, gh_o,
    hidden, w_in, embed, gain, w_head, tokens, mask,
    ctx_own, ctx_send, ctx_recv, cnt, cnt_recv, gath, scaled, gl, hs, r1, s1, r2, s2, r3,
    gc, ls1, ls1_r, ls2, ls2_r, ls3, ls3_r,
    in_sem, ctx_ss, ctx_rs, cnt_ss, cnt_rs, gc_ss, gc_rs,
    h1_ss, h1_rs, h2_ss, h2_rs, h3_ss, h3_rs, l_ss, l_rs,
):
    DP, T, S = sizes
    a, t, s = lax.axis_index("dp"), lax.axis_index("tensor"), lax.axis_index("seq")
    steps, nframes = tokens.shape
    frames = nframes // T
    width, vocab = w_head.shape
    rows = frames * steps
    piece = width // (DP * T * S)

    barrier = pltpu.get_barrier_semaphore()
    peers_t = [{"tensor": lax.rem(t + d, T)} for d in range(1, T)]
    peers_g = [
        {"dp": lax.rem(a + d, DP), "seq": lax.rem(s + e, S)}
        for d in range(DP)
        for e in range(S)
        if d or e
    ]
    for peer in peers_t + peers_g:
        pl.semaphore_signal(barrier, inc=1, device_id=peer, device_id_type=MESH)

    loads = [
        pltpu.make_async_copy(src, dst, in_sem.at[i])
        for i, (src, dst) in enumerate(
            [
                (hidden_h, hidden),
                (w_in_h, w_in),
                (mask_h, mask),
                (tokens_h, tokens),
                (embed_h, embed),
                (gain_h, gain),
                (w_head_h, w_head),
            ]
        )
    ]
    for load in loads:
        load.start()

    sends, seen = [], set()

    def got(copy):
        copy.wait_recv()
        seen.add(id(copy))

    def send(src, dst, ss, rs, peer):
        copy = pltpu.make_async_remote_copy(
            src_ref=src, dst_ref=dst, send_sem=ss, recv_sem=rs, device_id=peer, device_id_type=MESH
        )
        copy.start()
        sends.append(copy)
        return copy

    loads[0].wait()
    loads[1].wait()
    part = jnp.dot(hidden[...], w_in[...], preferred_element_type=F32).reshape(T, frames, width)
    ctx_send[...] = part.astype(BF16)
    ctx_own[...] = part
    loads[2].wait()
    mask_row = mask[...].astype(F32)
    cnt[...] = jnp.zeros(cnt.shape, F32) + jnp.sum(mask_row)
    pl.semaphore_wait(barrier, len(peers_t) + len(peers_g))
    ctx_copies = [
        send(ctx_send.at[lax.rem(t + d, T)], ctx_recv.at[d - 1], ctx_ss.at[d - 1], ctx_rs.at[d - 1],
             peers_t[d - 1])
        for d in range(1, T)
    ]
    cnt_copies = [
        send(cnt, cnt_recv.at[i], cnt_ss.at[i], cnt_rs.at[i], peer) for i, peer in enumerate(peers_g)
    ]

    loads[3].wait()
    spot = lax.broadcasted_iota(jnp.int32, (frames, nframes), 0) + t * frames
    here = lax.broadcasted_iota(jnp.int32, (frames, nframes), 1)
    mine = spot == here
    tok = tokens[...].astype(F32)
    lanes = lax.broadcasted_iota(jnp.int32, (frames, vocab), 1).astype(F32)
    hot = [
        jnp.sum(jnp.where(mine, tok[k : k + 1, :], 0.0), 1, keepdims=True) == lanes
        for k in range(steps)
    ]
    loads[4].wait()
    prev = jnp.concatenate([jnp.where(h, 1.0, 0.0).astype(BF16) for h in hot[:-1]], 0)
    gath[...] = jnp.dot(prev, embed[...], preferred_element_type=F32)
    mcol = jnp.sum(jnp.where(mine, mask_row, 0.0), 1, keepdims=True)
    loads[5].wait()
    loads[6].wait()
    gvec = gain[...]

    ctx = ctx_own[t]
    for d in range(1, T):
        got(ctx_copies[d - 1])
        ctx = ctx + ctx_recv[d - 1].astype(F32)
    ctx = ctx.astype(BF16).astype(F32)
    inputs = jnp.concatenate([ctx] * steps, 0) + jnp.concatenate(
        [jnp.zeros((frames, width), F32), gath[...]], 0
    )
    inverse = lax.rsqrt(jnp.mean(inputs * inputs, -1, keepdims=True) + 1e-06)
    normed = inputs * inverse
    flat = (normed * gvec).astype(BF16)
    scaled[...] = flat
    logits = jnp.dot(flat, w_head[...], preferred_element_type=F32)
    top = jnp.max(logits, -1, keepdims=True)
    powers = jnp.exp(logits - top)
    norm = jnp.sum(powers, -1, keepdims=True)
    total = top + jnp.log(norm)
    onehot = jnp.concatenate([jnp.where(h, 1.0, 0.0) for h in hot], 0)
    weights = jnp.concatenate([mcol] * steps, 0)
    nll = total - jnp.sum(logits * onehot, -1, keepdims=True)
    grads = ((powers * (1.0 / norm) - onehot) * weights).astype(BF16)
    gl[...] = grads

    chunk = width // DP
    order = []
    for j in range(DP - 1):
        up = jnp.where(j < a, j, j + 1)
        down = jnp.where(DP - 1 - j > a, DP - 1 - j, DP - 2 - j)
        order.append(jnp.where(2 * a < DP, down, up))
    order.append(a)
    h1 = []
    for j in range(DP):
        c = order[j]
        cols = scaled[:, pl.ds(pl.multiple_of(c * chunk, chunk), chunk)]
        term = lax.dot_general(
            cols, gl[...], (((0,), (0,)), ((), ())), preferred_element_type=F32
        )
        hs[j] = term.astype(BF16).reshape(T, S, piece, vocab)
        for e in range(1, S):
            h1.append(
                send(hs.at[j, :, lax.rem(s + e, S)], r1.at[j, e - 1], h1_ss.at[j, e - 1],
                     h1_rs.at[j, e - 1], {"seq": lax.rem(s + e, S)})
            )
    ls1[...] = jnp.zeros(ls1.shape, F32) + jnp.sum(weights * nll)
    n = 0
    lc1 = []
    for e in range(1, S):
        lc1.append(send(ls1, ls1_r.at[e - 1], l_ss.at[n], l_rs.at[n], {"seq": lax.rem(s + e, S)}))
        n += 1

    h2 = []
    for j in range(DP):
        acc = hs[j, :, s].astype(F32)
        for e in range(1, S):
            got(h1[j * (S - 1) + e - 1])
            acc = acc + r1[j, e - 1].astype(F32)
        s1[j] = acc.astype(BF16)
        for d in range(1, T):
            h2.append(
                send(s1.at[j, lax.rem(t + d, T)], r2.at[j, d - 1], h2_ss.at[j, d - 1],
                     h2_rs.at[j, d - 1], peers_t[d - 1])
            )
    lsum = ls1[...]
    for e in range(1, S):
        got(lc1[e - 1])
        lsum = lsum + ls1_r[e - 1]
    ls2[...] = lsum
    lc2 = []
    for d in range(1, T):
        lc2.append(send(ls2, ls2_r.at[d - 1], l_ss.at[n], l_rs.at[n], peers_t[d - 1]))
        n += 1

    grad_scaled = lax.dot_general(
        gl[...], w_head[...], (((1,), (1,)), ((), ())), preferred_element_type=F32
    )
    g = grad_scaled * gvec
    gi = inverse * (g - normed * jnp.mean(g * normed, -1, keepdims=True))
    gsum = gi[0:frames]
    for k in range(1, steps):
        gsum = gsum + gi[k * frames : (k + 1) * frames]
    gc[t] = gsum.astype(BF16)
    gc_copies = [
        send(gc.at[t], gc.at[t], gc_ss.at[d - 1], gc_rs.at[d - 1], peers_t[d - 1])
        for d in range(1, T)
    ]

    h3 = []
    for j in range(DP):
        acc = s1[j, t].astype(F32)
        for d in range(1, T):
            got(h2[j * (T - 1) + d - 1])
            acc = acc + r2[j, d - 1].astype(F32)
        if j < DP - 1:
            s2[j] = acc.astype(BF16)
            slot = lax.rem(order[j] - a + DP, DP) - 1
            h3.append(
                send(s2.at[j], r3.at[slot], h3_ss.at[j], h3_rs.at[slot], {"dp": order[j]})
            )
    lsum = ls2[...]
    for d in range(1, T):
        got(lc2[d - 1])
        lsum = lsum + ls2_r[d - 1]
    ls3[...] = lsum
    lc3 = []
    for d in range(1, DP):
        lc3.append(
            send(ls3, ls3_r.at[d - 1], l_ss.at[n], l_rs.at[n], {"dp": lax.rem(a + d, DP)})
        )
        n += 1
    total_mask = cnt[...]
    for i in range(len(peers_g)):
        got(cnt_copies[i])
        total_mask = total_mask + cnt_recv[i]
    share = 1.0 / (total_mask[0:1, 0:1] * steps)
    for d in range(1, T):
        got(gc_copies[d - 1])
    product = lax.dot_general(
        gc[...].reshape(nframes, width), w_in[...], (((1,), (1,)), ((), ())),
        preferred_element_type=F32,
    )
    gh_o[...] = (product * share).astype(BF16)

    for j in range(DP - 1):
        arrival = pltpu.make_async_remote_copy(
            src_ref=s2.at[j], dst_ref=r3.at[j], send_sem=h3_ss.at[j], recv_sem=h3_rs.at[j],
            device_id={"dp": lax.rem(a + 1, DP)}, device_id_type=MESH,
        )
        arrival.wait_recv()
        acc = acc + r3[j].astype(F32)
    acc = acc * share
    groups = vocab // 128
    for b in range(groups):
        head_o[pl.ds(b, piece, stride=groups), :] = acc[:, b * 128 : (b + 1) * 128]
    for d in range(1, DP):
        got(lc3[d - 1])
        lsum = lsum + ls3_r[d - 1]
    loss_o[...] = lsum[0:1, 0:1] * share
    for copy in sends:
        copy.wait_send()


def write_out(loss_i, head_i, gh_i, loss_o, head_o, gh_o, sem):
    copies = [
        pltpu.make_async_copy(src, dst, sem.at[i])
        for i, (src, dst) in enumerate([(gh_i, gh_o), (head_i, head_o), (loss_i, loss_o)])
    ]
    for copy in copies:
        copy.start()
    for copy in copies:
        copy.wait()


def per_device_kernel(hidden, w_in, embed, gain, w_head, tokens, frame_mask):
    DP, T, S = lax.axis_size("dp"), lax.axis_size("tensor"), lax.axis_size("seq")
    nframes, feats = hidden.shape
    steps = tokens.shape[1]
    frames = nframes // T
    width, vocab = w_head.shape
    rows = frames * steps
    piece = width // (DP * T * S)
    G = DP * S - 1
    V = pltpu.VMEM
    dma = pltpu.SemaphoreType.DMA
    scratch = [
        V(hidden.shape, BF16), V(w_in.shape, BF16), V(embed.shape, BF16), V((1, width), F32),
        V(w_head.shape, BF16), V((steps, nframes), jnp.int32), V((1, nframes), jnp.int32),
        V((T, frames, width), F32),
        V((T, frames, width), BF16),
        V((T - 1, frames, width), BF16),
        V((8, 128), F32),
        V((G, 8, 128), F32),
        V((rows - frames, width), F32),
        V((rows, width), BF16),
        V((rows, vocab), BF16),
        V((DP, T, S, piece, vocab), BF16),
        V((DP, S - 1, T, piece, vocab), BF16),
        V((DP, T, piece, vocab), BF16),
        V((DP, T - 1, piece, vocab), BF16),
        V((DP - 1, piece, vocab), BF16),
        V((DP - 1, piece, vocab), BF16),
        V((T, frames, width), BF16),
        V((8, 128), F32), V((S - 1, 8, 128), F32),
        V((8, 128), F32), V((T - 1, 8, 128), F32),
        V((8, 128), F32), V((DP - 1, 8, 128), F32),
        dma((7,)),
        dma((T - 1,)), dma((T - 1,)), dma((G,)), dma((G,)), dma((T - 1,)), dma((T - 1,)),
        dma((DP, S - 1)), dma((DP, S - 1)), dma((DP, T - 1)), dma((DP, T - 1)),
        dma((DP - 1,)), dma((DP - 1,)), dma((S + T + DP - 3,)), dma((S + T + DP - 3,)),
    ]
    shapes = (
        jax.ShapeDtypeStruct((1, 1), F32),
        jax.ShapeDtypeStruct((piece * vocab // 128, 128), F32),
        jax.ShapeDtypeStruct((nframes, feats), BF16),
    )
    vmem = pl.BlockSpec(memory_space=pltpu.VMEM)
    results = pl.pallas_call(
        functools.partial(kernel, (DP, T, S)),
        out_shape=shapes,
        in_specs=[pl.BlockSpec(memory_space=pltpu.HBM)] * 7,
        out_specs=(vmem, vmem, vmem),
        scratch_shapes=scratch,
        compiler_params=pltpu.CompilerParams(
            collective_id=0, has_side_effects=True, vmem_limit_bytes=40 << 20
        ),
        name="decode",
    )(*[pltpu.with_memory_space_constraint(x, pltpu.HBM) for x in (hidden, w_in, embed, gain.reshape(1, -1), w_head, tokens.T, frame_mask.reshape(1, -1))])
    loss, head, grad_hidden = pl.pallas_call(
        write_out,
        out_shape=shapes,
        in_specs=[pl.BlockSpec(memory_space=pl.ANY)] * 3,
        out_specs=(pl.BlockSpec(memory_space=pltpu.HBM),) * 3,
        scratch_shapes=[dma((3,))],
        compiler_params=pltpu.CompilerParams(vmem_limit_bytes=4 << 20),
        name="write_out",
    )(*results)
    return loss.reshape(()), head.reshape(-1), grad_hidden


def solution(mesh):
    def per_device(hidden, w_in, embed, gain, w_head, tokens, frame_mask):
        DP, T, S = mesh.shape["dp"], mesh.shape["tensor"], mesh.shape["seq"]
        width, vocab = w_head.shape
        fits = (
            width % (16 * DP * T * S) == 0
            and width % (128 * DP) == 0
            and vocab % 128 == 0
            and hidden.shape[0] % (16 * T) == 0
            and min(DP, T, S) > 1
        )
        run = per_device_kernel if fits else per_device_plain
        return run(hidden, w_in, embed, gain, w_head, tokens, frame_mask)

    placed = (
        P(("dp", "seq"), "tensor"),
        P("tensor", None),
        P(),
        P(),
        P(),
        P(("dp", "seq"), None),
        P(("dp", "seq")),
    )
    return jax.shard_map(
        per_device,
        mesh=mesh,
        in_specs=placed,
        out_specs=(P(), P(("dp", "tensor", "seq")), P(("dp", "seq"), "tensor")),
        check_vma=False,
    )
```

```python
import functools

import jax
import jax.numpy as jnp
from jax import lax
from jax.experimental import pallas as pl
from jax.experimental.pallas import tpu as pltpu
from jax.sharding import PartitionSpec as P

F32 = jnp.float32
BF16 = jnp.bfloat16
MESH = pl.DeviceIdType.MESH


def decode_terms(context, tok_rows, mask_rows, embed, gain, w_head, count_fn):
    frames = context.shape[0]
    width = context.shape[1]
    steps = tok_rows.shape[1]
    before = embed[tok_rows[:, :-1]].astype(jnp.float32)
    leading = jnp.zeros((frames, 1, width), jnp.float32)
    inputs = context.astype(jnp.float32)[:, None, :] + jnp.concatenate([leading, before], 1)
    inverse = lax.rsqrt(jnp.mean(inputs * inputs, -1, keepdims=True) + 1e-06)
    normed = inputs * inverse
    scaled = (normed * gain).astype(jnp.bfloat16)
    flat = scaled.reshape(frames * steps, width)
    logits = jnp.dot(flat, w_head, preferred_element_type=jnp.float32)
    top = jnp.max(logits, -1, keepdims=True)
    total = top[:, 0] + jnp.log(jnp.sum(jnp.exp(logits - top), -1))
    target = tok_rows.reshape(-1)
    onehot = (target[:, None] == jnp.arange(w_head.shape[1], dtype=jnp.int32)[None, :]).astype(
        jnp.float32
    )
    nll = total - jnp.sum(logits * onehot, -1)
    weights = (mask_rows.astype(jnp.float32)[:, None] * jnp.ones((1, steps), jnp.float32)).reshape(
        -1
    )
    count, loss_sum = count_fn(
        steps * jnp.sum(mask_rows.astype(jnp.float32)), jnp.sum(weights * nll)
    )
    probs = jnp.exp(logits - total[:, None])
    grad_logits = ((probs - onehot) * weights[:, None] / count).astype(jnp.bfloat16)
    head_term = lax.dot_general(
        flat, grad_logits, (((0,), (0,)), ((), ())), preferred_element_type=jnp.float32
    )
    grad_scaled = lax.dot_general(
        grad_logits, w_head, (((1,), (1,)), ((), ())), preferred_element_type=jnp.float32
    )
    scaled_grad = grad_scaled.reshape(inputs.shape) * gain
    grad_inputs = inverse * (
        scaled_grad - normed * jnp.mean(scaled_grad * normed, -1, keepdims=True)
    )
    grad_context = jnp.sum(grad_inputs, 1).astype(jnp.bfloat16)
    return (loss_sum / count, head_term, grad_context)


def add_totals(count_local, loss_local):
    return lax.psum((count_local, loss_local), ("dp", "tensor", "seq"))


def per_device_plain(hidden, w_in, embed, gain, w_head, tokens, frame_mask):
    groups = lax.axis_size("tensor")
    rows = hidden.shape[0] // groups
    context = lax.psum_scatter(
        jnp.dot(hidden, w_in, preferred_element_type=jnp.float32),
        "tensor",
        scatter_dimension=0,
        tiled=True,
    ).astype(jnp.bfloat16)
    offset = lax.axis_index("tensor") * rows
    tok_rows = lax.dynamic_slice_in_dim(tokens, offset, rows, 0)
    mask_rows = lax.dynamic_slice_in_dim(frame_mask, offset, rows, 0)
    loss, head_term, grad_context = decode_terms(
        context, tok_rows, mask_rows, embed, gain, w_head, add_totals
    )
    flat_term = head_term.reshape(-1)
    partial_grad = lax.psum_scatter(
        flat_term.astype(jnp.bfloat16), "dp", scatter_dimension=0, tiled=True
    ).astype(jnp.float32)
    grad_head = lax.psum_scatter(partial_grad, ("tensor", "seq"), scatter_dimension=0, tiled=True)
    product = lax.dot_general(
        lax.all_gather(grad_context, "tensor", axis=0, tiled=True),
        w_in,
        (((1,), (1,)), ((), ())),
        preferred_element_type=jnp.float32,
    )
    grad_hidden = product.astype(jnp.bfloat16)
    return (loss, grad_head, grad_hidden)


def kernel(
    sizes, hidden_h, w_in_h, embed_h, gain_h, w_head_h, tokens_h, mask_h,
    loss_o, head_o, gh_o,
    hidden, w_in, embed, gain, w_head, tokens, mask,
    ctx_own, ctx_send, ctx_recv, cnt, cnt_recv, gath, scaled, gl, hs, r1, s1, r2, s2, r3,
    gc, ls1, ls1_r, ls2, ls2_r, ls3, ls3_r,
    in_sem, ctx_ss, ctx_rs, cnt_ss, cnt_rs, gc_ss, gc_rs,
    h1_ss, h1_rs, h2_ss, h2_rs, h3_ss, h3_rs, l_ss, l_rs,
):
    DP, T, S = sizes
    a, t, s = lax.axis_index("dp"), lax.axis_index("tensor"), lax.axis_index("seq")
    steps, nframes = tokens.shape
    frames = nframes // T
    width, vocab = w_head.shape
    rows = frames * steps
    piece = width // (DP * T * S)

    barrier = pltpu.get_barrier_semaphore()
    peers_t = [{"tensor": lax.rem(t + d, T)} for d in range(1, T)]
    peers_g = [
        {"dp": lax.rem(a + d, DP), "seq": lax.rem(s + e, S)}
        for d in range(DP)
        for e in range(S)
        if d or e
    ]
    for peer in peers_t + peers_g:
        pl.semaphore_signal(barrier, inc=1, device_id=peer, device_id_type=MESH)

    loads = [
        pltpu.make_async_copy(src, dst, in_sem.at[i])
        for i, (src, dst) in enumerate(
            [
                (hidden_h, hidden),
                (w_in_h, w_in),
                (mask_h, mask),
                (tokens_h, tokens),
                (embed_h, embed),
                (gain_h, gain),
                (w_head_h, w_head),
            ]
        )
    ]
    for load in loads:
        load.start()

    sends, seen = [], set()

    def got(copy):
        copy.wait_recv()
        seen.add(id(copy))

    def send(src, dst, ss, rs, peer):
        copy = pltpu.make_async_remote_copy(
            src_ref=src, dst_ref=dst, send_sem=ss, recv_sem=rs, device_id=peer, device_id_type=MESH
        )
        copy.start()
        sends.append(copy)
        return copy

    loads[0].wait()
    loads[1].wait()
    part = jnp.dot(hidden[...], w_in[...], preferred_element_type=F32).reshape(T, frames, width)
    ctx_send[...] = part.astype(BF16)
    ctx_own[...] = part
    loads[2].wait()
    mask_row = mask[...].astype(F32)
    cnt[...] = jnp.zeros(cnt.shape, F32) + jnp.sum(mask_row)
    pl.semaphore_wait(barrier, len(peers_t) + len(peers_g))
    ctx_copies = [
        send(ctx_send.at[lax.rem(t + d, T)], ctx_recv.at[d - 1], ctx_ss.at[d - 1], ctx_rs.at[d - 1],
             peers_t[d - 1])
        for d in range(1, T)
    ]
    cnt_copies = [
        send(cnt, cnt_recv.at[i], cnt_ss.at[i], cnt_rs.at[i], peer) for i, peer in enumerate(peers_g)
    ]

    loads[3].wait()
    spot = lax.broadcasted_iota(jnp.int32, (frames, nframes), 0) + t * frames
    here = lax.broadcasted_iota(jnp.int32, (frames, nframes), 1)
    mine = spot == here
    tok = tokens[...].astype(F32)
    lanes = lax.broadcasted_iota(jnp.int32, (frames, vocab), 1).astype(F32)
    hot = [
        jnp.sum(jnp.where(mine, tok[k : k + 1, :], 0.0), 1, keepdims=True) == lanes
        for k in range(steps)
    ]
    loads[4].wait()
    prev = jnp.concatenate([jnp.where(h, 1.0, 0.0).astype(BF16) for h in hot[:-1]], 0)
    gath[...] = jnp.dot(prev, embed[...], preferred_element_type=F32)
    mcol = jnp.sum(jnp.where(mine, mask_row, 0.0), 1, keepdims=True)
    loads[5].wait()
    loads[6].wait()
    gvec = gain[...]

    ctx = ctx_own[t]
    for d in range(1, T):
        got(ctx_copies[d - 1])
        ctx = ctx + ctx_recv[d - 1].astype(F32)
    ctx = ctx.astype(BF16).astype(F32)
    inputs = jnp.concatenate([ctx] * steps, 0) + jnp.concatenate(
        [jnp.zeros((frames, width), F32), gath[...]], 0
    )
    inverse = lax.rsqrt(jnp.mean(inputs * inputs, -1, keepdims=True) + 1e-06)
    normed = inputs * inverse
    flat = (normed * gvec).astype(BF16)
    scaled[...] = flat
    logits = jnp.dot(flat, w_head[...], preferred_element_type=F32)
    top = jnp.max(logits, -1, keepdims=True)
    powers = jnp.exp(logits - top)
    norm = jnp.sum(powers, -1, keepdims=True)
    total = top + jnp.log(norm)
    onehot = jnp.concatenate([jnp.where(h, 1.0, 0.0) for h in hot], 0)
    weights = jnp.concatenate([mcol] * steps, 0)
    nll = total - jnp.sum(logits * onehot, -1, keepdims=True)
    grads = ((powers * (1.0 / norm) - onehot) * weights).astype(BF16)
    gl[...] = grads

    chunk = width // DP
    order = []
    for j in range(DP - 1):
        up = jnp.where(j < a, j, j + 1)
        down = jnp.where(DP - 1 - j > a, DP - 1 - j, DP - 2 - j)
        order.append(jnp.where(2 * a < DP, down, up))
    order.append(a)
    h1, h2 = [], []

    def tensor_stage(j):
        acc = hs[j, :, s].astype(F32)
        for e in range(1, S):
            got(h1[j * (S - 1) + e - 1])
            acc = acc + r1[j, e - 1].astype(F32)
        s1[j] = acc.astype(BF16)
        for d in range(1, T):
            h2.append(
                send(s1.at[j, lax.rem(t + d, T)], r2.at[j, d - 1], h2_ss.at[j, d - 1],
                     h2_rs.at[j, d - 1], peers_t[d - 1])
            )

    lag = 2
    for j in range(DP):
        c = order[j]
        cols = scaled[:, pl.ds(pl.multiple_of(c * chunk, chunk), chunk)]
        term = lax.dot_general(
            cols, gl[...], (((0,), (0,)), ((), ())), preferred_element_type=F32
        )
        hs[j] = term.astype(BF16).reshape(T, S, piece, vocab)
        for e in range(1, S):
            h1.append(
                send(hs.at[j, :, lax.rem(s + e, S)], r1.at[j, e - 1], h1_ss.at[j, e - 1],
                     h1_rs.at[j, e - 1], {"seq": lax.rem(s + e, S)})
            )
        if j >= lag:
            tensor_stage(j - lag)
    for j in range(max(DP - lag, 0), DP):
        tensor_stage(j)
    ls1[...] = jnp.zeros(ls1.shape, F32) + jnp.sum(weights * nll)
    n = 0
    lc1 = []
    for e in range(1, S):
        lc1.append(send(ls1, ls1_r.at[e - 1], l_ss.at[n], l_rs.at[n], {"seq": lax.rem(s + e, S)}))
        n += 1

    lsum = ls1[...]
    for e in range(1, S):
        got(lc1[e - 1])
        lsum = lsum + ls1_r[e - 1]
    ls2[...] = lsum
    lc2 = []
    for d in range(1, T):
        lc2.append(send(ls2, ls2_r.at[d - 1], l_ss.at[n], l_rs.at[n], peers_t[d - 1]))
        n += 1

    grad_scaled = lax.dot_general(
        gl[...], w_head[...], (((1,), (1,)), ((), ())), preferred_element_type=F32
    )
    g = grad_scaled * gvec
    gi = inverse * (g - normed * jnp.mean(g * normed, -1, keepdims=True))
    gsum = gi[0:frames]
    for k in range(1, steps):
        gsum = gsum + gi[k * frames : (k + 1) * frames]
    gc[t] = gsum.astype(BF16)
    gc_copies = [
        send(gc.at[t], gc.at[t], gc_ss.at[d - 1], gc_rs.at[d - 1], peers_t[d - 1])
        for d in range(1, T)
    ]

    h3 = []
    for j in range(DP):
        acc = s1[j, t].astype(F32)
        for d in range(1, T):
            got(h2[j * (T - 1) + d - 1])
            acc = acc + r2[j, d - 1].astype(F32)
        if j < DP - 1:
            s2[j] = acc.astype(BF16)
            slot = lax.rem(order[j] - a + DP, DP) - 1
            h3.append(
                send(s2.at[j], r3.at[slot], h3_ss.at[j], h3_rs.at[slot], {"dp": order[j]})
            )
    lsum = ls2[...]
    for d in range(1, T):
        got(lc2[d - 1])
        lsum = lsum + ls2_r[d - 1]
    ls3[...] = lsum
    lc3 = []
    for d in range(1, DP):
        lc3.append(
            send(ls3, ls3_r.at[d - 1], l_ss.at[n], l_rs.at[n], {"dp": lax.rem(a + d, DP)})
        )
        n += 1
    total_mask = cnt[...]
    for i in range(len(peers_g)):
        got(cnt_copies[i])
        total_mask = total_mask + cnt_recv[i]
    share = 1.0 / (total_mask[0:1, 0:1] * steps)
    for d in range(1, T):
        got(gc_copies[d - 1])
    product = lax.dot_general(
        gc[...].reshape(nframes, width), w_in[...], (((1,), (1,)), ((), ())),
        preferred_element_type=F32,
    )
    gh_o[...] = (product * share).astype(BF16)

    for j in range(DP - 1):
        arrival = pltpu.make_async_remote_copy(
            src_ref=s2.at[j], dst_ref=r3.at[j], send_sem=h3_ss.at[j], recv_sem=h3_rs.at[j],
            device_id={"dp": lax.rem(a + 1, DP)}, device_id_type=MESH,
        )
        arrival.wait_recv()
        acc = acc + r3[j].astype(F32)
    acc = acc * share
    groups = vocab // 128
    for b in range(groups):
        head_o[pl.ds(b, piece, stride=groups), :] = acc[:, b * 128 : (b + 1) * 128]
    for d in range(1, DP):
        got(lc3[d - 1])
        lsum = lsum + ls3_r[d - 1]
    loss_o[...] = lsum[0:1, 0:1] * share
    for copy in sends:
        copy.wait_send()


def write_out(loss_i, head_i, gh_i, loss_o, head_o, gh_o, sem):
    copies = [
        pltpu.make_async_copy(src, dst, sem.at[i])
        for i, (src, dst) in enumerate([(gh_i, gh_o), (head_i, head_o), (loss_i, loss_o)])
    ]
    for copy in copies:
        copy.start()
    for copy in copies:
        copy.wait()


def per_device_kernel(hidden, w_in, embed, gain, w_head, tokens, frame_mask):
    DP, T, S = lax.axis_size("dp"), lax.axis_size("tensor"), lax.axis_size("seq")
    nframes, feats = hidden.shape
    steps = tokens.shape[1]
    frames = nframes // T
    width, vocab = w_head.shape
    rows = frames * steps
    piece = width // (DP * T * S)
    G = DP * S - 1
    V = pltpu.VMEM
    dma = pltpu.SemaphoreType.DMA
    scratch = [
        V(hidden.shape, BF16), V(w_in.shape, BF16), V(embed.shape, BF16), V((1, width), F32),
        V(w_head.shape, BF16), V((steps, nframes), jnp.int32), V((1, nframes), jnp.int32),
        V((T, frames, width), F32),
        V((T, frames, width), BF16),
        V((T - 1, frames, width), BF16),
        V((8, 128), F32),
        V((G, 8, 128), F32),
        V((rows - frames, width), F32),
        V((rows, width), BF16),
        V((rows, vocab), BF16),
        V((DP, T, S, piece, vocab), BF16),
        V((DP, S - 1, T, piece, vocab), BF16),
        V((DP, T, piece, vocab), BF16),
        V((DP, T - 1, piece, vocab), BF16),
        V((DP - 1, piece, vocab), BF16),
        V((DP - 1, piece, vocab), BF16),
        V((T, frames, width), BF16),
        V((8, 128), F32), V((S - 1, 8, 128), F32),
        V((8, 128), F32), V((T - 1, 8, 128), F32),
        V((8, 128), F32), V((DP - 1, 8, 128), F32),
        dma((7,)),
        dma((T - 1,)), dma((T - 1,)), dma((G,)), dma((G,)), dma((T - 1,)), dma((T - 1,)),
        dma((DP, S - 1)), dma((DP, S - 1)), dma((DP, T - 1)), dma((DP, T - 1)),
        dma((DP - 1,)), dma((DP - 1,)), dma((S + T + DP - 3,)), dma((S + T + DP - 3,)),
    ]
    shapes = (
        jax.ShapeDtypeStruct((1, 1), F32),
        jax.ShapeDtypeStruct((piece * vocab // 128, 128), F32),
        jax.ShapeDtypeStruct((nframes, feats), BF16),
    )
    vmem = pl.BlockSpec(memory_space=pltpu.VMEM)
    results = pl.pallas_call(
        functools.partial(kernel, (DP, T, S)),
        out_shape=shapes,
        in_specs=[pl.BlockSpec(memory_space=pltpu.HBM)] * 7,
        out_specs=(vmem, vmem, vmem),
        scratch_shapes=scratch,
        compiler_params=pltpu.CompilerParams(
            collective_id=0, has_side_effects=True, vmem_limit_bytes=40 << 20
        ),
        name="decode",
    )(*[pltpu.with_memory_space_constraint(x, pltpu.HBM) for x in (hidden, w_in, embed, gain.reshape(1, -1), w_head, tokens.T, frame_mask.reshape(1, -1))])
    loss, head, grad_hidden = pl.pallas_call(
        write_out,
        out_shape=shapes,
        in_specs=[pl.BlockSpec(memory_space=pl.ANY)] * 3,
        out_specs=(pl.BlockSpec(memory_space=pltpu.HBM),) * 3,
        scratch_shapes=[dma((3,))],
        compiler_params=pltpu.CompilerParams(vmem_limit_bytes=4 << 20),
        name="write_out",
    )(*results)
    return loss.reshape(()), head.reshape(-1), grad_hidden


def solution(mesh):
    def per_device(hidden, w_in, embed, gain, w_head, tokens, frame_mask):
        DP, T, S = mesh.shape["dp"], mesh.shape["tensor"], mesh.shape["seq"]
        width, vocab = w_head.shape
        fits = (
            width % (16 * DP * T * S) == 0
            and width % (128 * DP) == 0
            and vocab % 128 == 0
            and hidden.shape[0] % (16 * T) == 0
            and min(DP, T, S) > 1
        )
        run = per_device_kernel if fits else per_device_plain
        return run(hidden, w_in, embed, gain, w_head, tokens, frame_mask)

    placed = (
        P(("dp", "seq"), "tensor"),
        P("tensor", None),
        P(),
        P(),
        P(),
        P(("dp", "seq"), None),
        P(("dp", "seq")),
    )
    return jax.shard_map(
        per_device,
        mesh=mesh,
        in_specs=placed,
        out_specs=(P(), P(("dp", "tensor", "seq")), P(("dp", "seq"), "tensor")),
        check_vma=False,
    )
```

```python
import functools

import jax
import jax.numpy as jnp
from jax import lax
from jax.experimental import pallas as pl
from jax.experimental.pallas import tpu as pltpu
from jax.sharding import PartitionSpec as P

F32 = jnp.float32
BF16 = jnp.bfloat16
MESH = pl.DeviceIdType.MESH


def decode_terms(context, tok_rows, mask_rows, embed, gain, w_head, count_fn):
    frames = context.shape[0]
    width = context.shape[1]
    steps = tok_rows.shape[1]
    before = embed[tok_rows[:, :-1]].astype(jnp.float32)
    leading = jnp.zeros((frames, 1, width), jnp.float32)
    inputs = context.astype(jnp.float32)[:, None, :] + jnp.concatenate([leading, before], 1)
    inverse = lax.rsqrt(jnp.mean(inputs * inputs, -1, keepdims=True) + 1e-06)
    normed = inputs * inverse
    scaled = (normed * gain).astype(jnp.bfloat16)
    flat = scaled.reshape(frames * steps, width)
    logits = jnp.dot(flat, w_head, preferred_element_type=jnp.float32)
    top = jnp.max(logits, -1, keepdims=True)
    total = top[:, 0] + jnp.log(jnp.sum(jnp.exp(logits - top), -1))
    target = tok_rows.reshape(-1)
    onehot = (target[:, None] == jnp.arange(w_head.shape[1], dtype=jnp.int32)[None, :]).astype(
        jnp.float32
    )
    nll = total - jnp.sum(logits * onehot, -1)
    weights = (mask_rows.astype(jnp.float32)[:, None] * jnp.ones((1, steps), jnp.float32)).reshape(
        -1
    )
    count, loss_sum = count_fn(
        steps * jnp.sum(mask_rows.astype(jnp.float32)), jnp.sum(weights * nll)
    )
    probs = jnp.exp(logits - total[:, None])
    grad_logits = ((probs - onehot) * weights[:, None] / count).astype(jnp.bfloat16)
    head_term = lax.dot_general(
        flat, grad_logits, (((0,), (0,)), ((), ())), preferred_element_type=jnp.float32
    )
    grad_scaled = lax.dot_general(
        grad_logits, w_head, (((1,), (1,)), ((), ())), preferred_element_type=jnp.float32
    )
    scaled_grad = grad_scaled.reshape(inputs.shape) * gain
    grad_inputs = inverse * (
        scaled_grad - normed * jnp.mean(scaled_grad * normed, -1, keepdims=True)
    )
    grad_context = jnp.sum(grad_inputs, 1).astype(jnp.bfloat16)
    return (loss_sum / count, head_term, grad_context)


def add_totals(count_local, loss_local):
    return lax.psum((count_local, loss_local), ("dp", "tensor", "seq"))


def per_device_plain(hidden, w_in, embed, gain, w_head, tokens, frame_mask):
    groups = lax.axis_size("tensor")
    rows = hidden.shape[0] // groups
    context = lax.psum_scatter(
        jnp.dot(hidden, w_in, preferred_element_type=jnp.float32),
        "tensor",
        scatter_dimension=0,
        tiled=True,
    ).astype(jnp.bfloat16)
    offset = lax.axis_index("tensor") * rows
    tok_rows = lax.dynamic_slice_in_dim(tokens, offset, rows, 0)
    mask_rows = lax.dynamic_slice_in_dim(frame_mask, offset, rows, 0)
    loss, head_term, grad_context = decode_terms(
        context, tok_rows, mask_rows, embed, gain, w_head, add_totals
    )
    flat_term = head_term.reshape(-1)
    partial_grad = lax.psum_scatter(
        flat_term.astype(jnp.bfloat16), "dp", scatter_dimension=0, tiled=True
    ).astype(jnp.float32)
    grad_head = lax.psum_scatter(partial_grad, ("tensor", "seq"), scatter_dimension=0, tiled=True)
    product = lax.dot_general(
        lax.all_gather(grad_context, "tensor", axis=0, tiled=True),
        w_in,
        (((1,), (1,)), ((), ())),
        preferred_element_type=jnp.float32,
    )
    grad_hidden = product.astype(jnp.bfloat16)
    return (loss, grad_head, grad_hidden)


def kernel(
    sizes, hidden_h, w_in_h, embed_h, gain_h, w_head_h, tokens_h, mask_h,
    loss_o, head_o, gh_o,
    hidden, w_in, embed, gain, w_head, tokens, mask,
    ctx_own, ctx_send, ctx_recv, cnt, cnt_recv, gath, scaled, gl, hs, r1, s1, r2, s2, r3,
    gc, ls1, ls1_r, ls2, ls2_r, ls3, ls3_r,
    in_sem, ctx_ss, ctx_rs, cnt_ss, cnt_rs, gc_ss, gc_rs,
    h1_ss, h1_rs, h2_ss, h2_rs, h3_ss, h3_rs, l_ss, l_rs,
):
    DP, T, S = sizes
    a, t, s = lax.axis_index("dp"), lax.axis_index("tensor"), lax.axis_index("seq")
    steps, nframes = tokens.shape
    frames = nframes // T
    width, vocab = w_head.shape
    rows = frames * steps
    piece = width // (DP * T * S)

    barrier = pltpu.get_barrier_semaphore()
    peers_t = [{"tensor": lax.rem(t + d, T)} for d in range(1, T)]
    peers_g = [
        {"dp": lax.rem(a + d, DP), "seq": lax.rem(s + e, S)}
        for d in range(DP)
        for e in range(S)
        if d or e
    ]
    for peer in peers_t + peers_g:
        pl.semaphore_signal(barrier, inc=1, device_id=peer, device_id_type=MESH)

    loads = [
        pltpu.make_async_copy(src, dst, in_sem.at[i])
        for i, (src, dst) in enumerate(
            [
                (hidden_h, hidden),
                (w_in_h, w_in),
                (mask_h, mask),
                (tokens_h, tokens),
                (embed_h, embed),
                (gain_h, gain),
                (w_head_h, w_head),
            ]
        )
    ]
    for load in loads:
        load.start()

    sends, seen = [], set()

    def got(copy):
        copy.wait_recv()
        seen.add(id(copy))

    def send(src, dst, ss, rs, peer):
        copy = pltpu.make_async_remote_copy(
            src_ref=src, dst_ref=dst, send_sem=ss, recv_sem=rs, device_id=peer, device_id_type=MESH
        )
        copy.start()
        sends.append(copy)
        return copy

    loads[0].wait()
    loads[1].wait()
    part = jnp.dot(hidden[...], w_in[...], preferred_element_type=F32).reshape(T, frames, width)
    ctx_send[...] = part.astype(BF16)
    ctx_own[...] = part
    loads[2].wait()
    mask_row = mask[...].astype(F32)
    cnt[...] = jnp.zeros(cnt.shape, F32) + jnp.sum(mask_row)
    pl.semaphore_wait(barrier, len(peers_t) + len(peers_g))
    ctx_copies = [
        send(ctx_send.at[lax.rem(t + d, T)], ctx_recv.at[d - 1], ctx_ss.at[d - 1], ctx_rs.at[d - 1],
             peers_t[d - 1])
        for d in range(1, T)
    ]
    cnt_copies = [
        send(cnt, cnt_recv.at[i], cnt_ss.at[i], cnt_rs.at[i], peer) for i, peer in enumerate(peers_g)
    ]

    loads[3].wait()
    spot = lax.broadcasted_iota(jnp.int32, (frames, nframes), 0) + t * frames
    here = lax.broadcasted_iota(jnp.int32, (frames, nframes), 1)
    mine = spot == here
    tok = tokens[...].astype(F32)
    lanes = lax.broadcasted_iota(jnp.int32, (frames, vocab), 1).astype(F32)
    hot = [
        jnp.sum(jnp.where(mine, tok[k : k + 1, :], 0.0), 1, keepdims=True) == lanes
        for k in range(steps)
    ]
    loads[4].wait()
    prev = jnp.concatenate([jnp.where(h, 1.0, 0.0).astype(BF16) for h in hot[:-1]], 0)
    gath[...] = jnp.dot(prev, embed[...], preferred_element_type=F32)
    mcol = jnp.sum(jnp.where(mine, mask_row, 0.0), 1, keepdims=True)
    loads[5].wait()
    loads[6].wait()
    gvec = gain[...]

    ctx = ctx_own[t]
    for d in range(1, T):
        got(ctx_copies[d - 1])
        ctx = ctx + ctx_recv[d - 1].astype(F32)
    ctx = ctx.astype(BF16).astype(F32)
    inputs = jnp.concatenate([ctx] * steps, 0) + jnp.concatenate(
        [jnp.zeros((frames, width), F32), gath[...]], 0
    )
    inverse = lax.rsqrt(jnp.mean(inputs * inputs, -1, keepdims=True) + 1e-06)
    normed = inputs * inverse
    flat = (normed * gvec).astype(BF16)
    scaled[...] = flat
    logits = jnp.dot(flat, w_head[...], preferred_element_type=F32)
    top = jnp.max(logits, -1, keepdims=True)
    powers = jnp.exp(logits - top)
    norm = jnp.sum(powers, -1, keepdims=True)
    total = top + jnp.log(norm)
    onehot = jnp.concatenate([jnp.where(h, 1.0, 0.0) for h in hot], 0)
    weights = jnp.concatenate([mcol] * steps, 0)
    nll = total - jnp.sum(logits * onehot, -1, keepdims=True)
    grads = ((powers * (1.0 / norm) - onehot) * weights).astype(BF16)
    gl[...] = grads

    chunk = width // DP
    order = [lax.rem(a + 1 + j, DP) for j in range(DP)]
    h1, h2 = [], []

    def tensor_stage(j):
        acc = hs[j, :, s].astype(F32)
        for e in range(1, S):
            got(h1[j * (S - 1) + e - 1])
            acc = acc + r1[j, e - 1].astype(F32)
        s1[j] = acc.astype(BF16)
        for d in range(1, T):
            h2.append(
                send(s1.at[j, lax.rem(t + d, T)], r2.at[j, d - 1], h2_ss.at[j, d - 1],
                     h2_rs.at[j, d - 1], peers_t[d - 1])
            )

    lag = 2
    for j in range(DP):
        c = order[j]
        cols = scaled[:, pl.ds(pl.multiple_of(c * chunk, chunk), chunk)]
        term = lax.dot_general(
            cols, gl[...], (((0,), (0,)), ((), ())), preferred_element_type=F32
        )
        hs[j] = term.astype(BF16).reshape(T, S, piece, vocab)
        for e in range(1, S):
            h1.append(
                send(hs.at[j, :, lax.rem(s + e, S)], r1.at[j, e - 1], h1_ss.at[j, e - 1],
                     h1_rs.at[j, e - 1], {"seq": lax.rem(s + e, S)})
            )
        if j >= lag:
            tensor_stage(j - lag)
    for j in range(max(DP - lag, 0), DP):
        tensor_stage(j)
    ls1[...] = jnp.zeros(ls1.shape, F32) + jnp.sum(weights * nll)
    n = 0
    lc1 = []
    for e in range(1, S):
        lc1.append(send(ls1, ls1_r.at[e - 1], l_ss.at[n], l_rs.at[n], {"seq": lax.rem(s + e, S)}))
        n += 1

    lsum = ls1[...]
    for e in range(1, S):
        got(lc1[e - 1])
        lsum = lsum + ls1_r[e - 1]
    ls2[...] = lsum
    lc2 = []
    for d in range(1, T):
        lc2.append(send(ls2, ls2_r.at[d - 1], l_ss.at[n], l_rs.at[n], peers_t[d - 1]))
        n += 1

    grad_scaled = lax.dot_general(
        gl[...], w_head[...], (((1,), (1,)), ((), ())), preferred_element_type=F32
    )
    g = grad_scaled * gvec
    gi = inverse * (g - normed * jnp.mean(g * normed, -1, keepdims=True))
    gsum = gi[0:frames]
    for k in range(1, steps):
        gsum = gsum + gi[k * frames : (k + 1) * frames]
    gc[t] = gsum.astype(BF16)
    gc_copies = [
        send(gc.at[t], gc.at[t], gc_ss.at[d - 1], gc_rs.at[d - 1], peers_t[d - 1])
        for d in range(1, T)
    ]

    h3 = []
    for j in range(DP):
        acc = s1[j, t].astype(F32)
        for d in range(1, T):
            got(h2[j * (T - 1) + d - 1])
            acc = acc + r2[j, d - 1].astype(F32)
        if j < DP - 1:
            s2[j] = acc.astype(BF16)
            slot = lax.rem(order[j] - a + DP, DP) - 1
            h3.append(
                send(s2.at[j], r3.at[slot], h3_ss.at[j], h3_rs.at[slot], {"dp": order[j]})
            )
    lsum = ls2[...]
    for d in range(1, T):
        got(lc2[d - 1])
        lsum = lsum + ls2_r[d - 1]
    ls3[...] = lsum
    lc3 = []
    for d in range(1, DP):
        lc3.append(
            send(ls3, ls3_r.at[d - 1], l_ss.at[n], l_rs.at[n], {"dp": lax.rem(a + d, DP)})
        )
        n += 1
    total_mask = cnt[...]
    for i in range(len(peers_g)):
        got(cnt_copies[i])
        total_mask = total_mask + cnt_recv[i]
    share = 1.0 / (total_mask[0:1, 0:1] * steps)
    for d in range(1, T):
        got(gc_copies[d - 1])
    product = lax.dot_general(
        gc[...].reshape(nframes, width), w_in[...], (((1,), (1,)), ((), ())),
        preferred_element_type=F32,
    )
    gh_o[...] = (product * share).astype(BF16)

    for j in range(DP - 1):
        arrival = pltpu.make_async_remote_copy(
            src_ref=s2.at[j], dst_ref=r3.at[j], send_sem=h3_ss.at[j], recv_sem=h3_rs.at[j],
            device_id={"dp": lax.rem(a + 1, DP)}, device_id_type=MESH,
        )
        arrival.wait_recv()
        acc = acc + r3[j].astype(F32)
    acc = acc * share
    groups = vocab // 128
    for b in range(groups):
        head_o[pl.ds(b, piece, stride=groups), :] = acc[:, b * 128 : (b + 1) * 128]
    for d in range(1, DP):
        got(lc3[d - 1])
        lsum = lsum + ls3_r[d - 1]
    loss_o[...] = lsum[0:1, 0:1] * share
    for copy in sends:
        copy.wait_send()


def write_out(loss_i, head_i, gh_i, loss_o, head_o, gh_o, sem):
    copies = [
        pltpu.make_async_copy(src, dst, sem.at[i])
        for i, (src, dst) in enumerate([(gh_i, gh_o), (head_i, head_o), (loss_i, loss_o)])
    ]
    for copy in copies:
        copy.start()
    for copy in copies:
        copy.wait()


def per_device_kernel(hidden, w_in, embed, gain, w_head, tokens, frame_mask):
    DP, T, S = lax.axis_size("dp"), lax.axis_size("tensor"), lax.axis_size("seq")
    nframes, feats = hidden.shape
    steps = tokens.shape[1]
    frames = nframes // T
    width, vocab = w_head.shape
    rows = frames * steps
    piece = width // (DP * T * S)
    G = DP * S - 1
    V = pltpu.VMEM
    dma = pltpu.SemaphoreType.DMA
    scratch = [
        V(hidden.shape, BF16), V(w_in.shape, BF16), V(embed.shape, BF16), V((1, width), F32),
        V(w_head.shape, BF16), V((steps, nframes), jnp.int32), V((1, nframes), jnp.int32),
        V((T, frames, width), F32),
        V((T, frames, width), BF16),
        V((T - 1, frames, width), BF16),
        V((8, 128), F32),
        V((G, 8, 128), F32),
        V((rows - frames, width), F32),
        V((rows, width), BF16),
        V((rows, vocab), BF16),
        V((DP, T, S, piece, vocab), BF16),
        V((DP, S - 1, T, piece, vocab), BF16),
        V((DP, T, piece, vocab), BF16),
        V((DP, T - 1, piece, vocab), BF16),
        V((DP - 1, piece, vocab), BF16),
        V((DP - 1, piece, vocab), BF16),
        V((T, frames, width), BF16),
        V((8, 128), F32), V((S - 1, 8, 128), F32),
        V((8, 128), F32), V((T - 1, 8, 128), F32),
        V((8, 128), F32), V((DP - 1, 8, 128), F32),
        dma((7,)),
        dma((T - 1,)), dma((T - 1,)), dma((G,)), dma((G,)), dma((T - 1,)), dma((T - 1,)),
        dma((DP, S - 1)), dma((DP, S - 1)), dma((DP, T - 1)), dma((DP, T - 1)),
        dma((DP - 1,)), dma((DP - 1,)), dma((S + T + DP - 3,)), dma((S + T + DP - 3,)),
    ]
    shapes = (
        jax.ShapeDtypeStruct((1, 1), F32),
        jax.ShapeDtypeStruct((piece * vocab // 128, 128), F32),
        jax.ShapeDtypeStruct((nframes, feats), BF16),
    )
    vmem = pl.BlockSpec(memory_space=pltpu.VMEM)
    results = pl.pallas_call(
        functools.partial(kernel, (DP, T, S)),
        out_shape=shapes,
        in_specs=[pl.BlockSpec(memory_space=pltpu.HBM)] * 7,
        out_specs=(vmem, vmem, vmem),
        scratch_shapes=scratch,
        compiler_params=pltpu.CompilerParams(
            collective_id=0, has_side_effects=True, vmem_limit_bytes=40 << 20
        ),
        name="decode",
    )(*[pltpu.with_memory_space_constraint(x, pltpu.HBM) for x in (hidden, w_in, embed, gain.reshape(1, -1), w_head, tokens.T, frame_mask.reshape(1, -1))])
    loss, head, grad_hidden = pl.pallas_call(
        write_out,
        out_shape=shapes,
        in_specs=[pl.BlockSpec(memory_space=pl.ANY)] * 3,
        out_specs=(pl.BlockSpec(memory_space=pltpu.HBM),) * 3,
        scratch_shapes=[dma((3,))],
        compiler_params=pltpu.CompilerParams(vmem_limit_bytes=4 << 20),
        name="write_out",
    )(*results)
    return loss.reshape(()), head.reshape(-1), grad_hidden


def solution(mesh):
    def per_device(hidden, w_in, embed, gain, w_head, tokens, frame_mask):
        DP, T, S = mesh.shape["dp"], mesh.shape["tensor"], mesh.shape["seq"]
        width, vocab = w_head.shape
        fits = (
            width % (16 * DP * T * S) == 0
            and width % (128 * DP) == 0
            and vocab % 128 == 0
            and hidden.shape[0] % (16 * T) == 0
            and min(DP, T, S) > 1
        )
        run = per_device_kernel if fits else per_device_plain
        return run(hidden, w_in, embed, gain, w_head, tokens, frame_mask)

    placed = (
        P(("dp", "seq"), "tensor"),
        P("tensor", None),
        P(),
        P(),
        P(),
        P(("dp", "seq"), None),
        P(("dp", "seq")),
    )
    return jax.shard_map(
        per_device,
        mesh=mesh,
        in_specs=placed,
        out_specs=(P(), P(("dp", "tensor", "seq")), P(("dp", "seq"), "tensor")),
        check_vma=False,
    )
```

```python
import functools

import jax
import jax.numpy as jnp
from jax import lax
from jax.experimental import pallas as pl
from jax.experimental.pallas import tpu as pltpu
from jax.sharding import PartitionSpec as P

F32 = jnp.float32
BF16 = jnp.bfloat16
MESH = pl.DeviceIdType.MESH


def decode_terms(context, tok_rows, mask_rows, embed, gain, w_head, count_fn):
    frames = context.shape[0]
    width = context.shape[1]
    steps = tok_rows.shape[1]
    before = embed[tok_rows[:, :-1]].astype(jnp.float32)
    leading = jnp.zeros((frames, 1, width), jnp.float32)
    inputs = context.astype(jnp.float32)[:, None, :] + jnp.concatenate([leading, before], 1)
    inverse = lax.rsqrt(jnp.mean(inputs * inputs, -1, keepdims=True) + 1e-06)
    normed = inputs * inverse
    scaled = (normed * gain).astype(jnp.bfloat16)
    flat = scaled.reshape(frames * steps, width)
    logits = jnp.dot(flat, w_head, preferred_element_type=jnp.float32)
    top = jnp.max(logits, -1, keepdims=True)
    total = top[:, 0] + jnp.log(jnp.sum(jnp.exp(logits - top), -1))
    target = tok_rows.reshape(-1)
    onehot = (target[:, None] == jnp.arange(w_head.shape[1], dtype=jnp.int32)[None, :]).astype(
        jnp.float32
    )
    nll = total - jnp.sum(logits * onehot, -1)
    weights = (mask_rows.astype(jnp.float32)[:, None] * jnp.ones((1, steps), jnp.float32)).reshape(
        -1
    )
    count, loss_sum = count_fn(
        steps * jnp.sum(mask_rows.astype(jnp.float32)), jnp.sum(weights * nll)
    )
    probs = jnp.exp(logits - total[:, None])
    grad_logits = ((probs - onehot) * weights[:, None] / count).astype(jnp.bfloat16)
    head_term = lax.dot_general(
        flat, grad_logits, (((0,), (0,)), ((), ())), preferred_element_type=jnp.float32
    )
    grad_scaled = lax.dot_general(
        grad_logits, w_head, (((1,), (1,)), ((), ())), preferred_element_type=jnp.float32
    )
    scaled_grad = grad_scaled.reshape(inputs.shape) * gain
    grad_inputs = inverse * (
        scaled_grad - normed * jnp.mean(scaled_grad * normed, -1, keepdims=True)
    )
    grad_context = jnp.sum(grad_inputs, 1).astype(jnp.bfloat16)
    return (loss_sum / count, head_term, grad_context)


def add_totals(count_local, loss_local):
    return lax.psum((count_local, loss_local), ("dp", "tensor", "seq"))


def per_device_plain(hidden, w_in, embed, gain, w_head, tokens, frame_mask):
    groups = lax.axis_size("tensor")
    rows = hidden.shape[0] // groups
    context = lax.psum_scatter(
        jnp.dot(hidden, w_in, preferred_element_type=jnp.float32),
        "tensor",
        scatter_dimension=0,
        tiled=True,
    ).astype(jnp.bfloat16)
    offset = lax.axis_index("tensor") * rows
    tok_rows = lax.dynamic_slice_in_dim(tokens, offset, rows, 0)
    mask_rows = lax.dynamic_slice_in_dim(frame_mask, offset, rows, 0)
    loss, head_term, grad_context = decode_terms(
        context, tok_rows, mask_rows, embed, gain, w_head, add_totals
    )
    flat_term = head_term.reshape(-1)
    partial_grad = lax.psum_scatter(
        flat_term.astype(jnp.bfloat16), "dp", scatter_dimension=0, tiled=True
    ).astype(jnp.float32)
    grad_head = lax.psum_scatter(partial_grad, ("tensor", "seq"), scatter_dimension=0, tiled=True)
    product = lax.dot_general(
        lax.all_gather(grad_context, "tensor", axis=0, tiled=True),
        w_in,
        (((1,), (1,)), ((), ())),
        preferred_element_type=jnp.float32,
    )
    grad_hidden = product.astype(jnp.bfloat16)
    return (loss, grad_head, grad_hidden)


def kernel(
    sizes, hidden_h, w_in_h, embed_h, gain_h, w_head_h, tokens_h, mask_h,
    loss_o, head_o, gh_o,
    hidden, w_in, embed, gain, w_head, tokens, mask,
    ctx_own, ctx_send, ctx_recv, cnt, cnt_recv, gath, scaled, gl, hs, r1, s1, r2, s2, r3,
    gc, ls1, ls1_r, ls2, ls2_r, ls3, ls3_r,
    in_sem, ctx_ss, ctx_rs, cnt_ss, cnt_rs, gc_ss, gc_rs,
    h1_ss, h1_rs, h2_ss, h2_rs, h3_ss, h3_rs, l_ss, l_rs,
):
    DP, T, S = sizes
    a, t, s = lax.axis_index("dp"), lax.axis_index("tensor"), lax.axis_index("seq")
    steps, nframes = tokens.shape
    frames = nframes // T
    width, vocab = w_head.shape
    rows = frames * steps
    piece = width // (DP * T * S)

    barrier = pltpu.get_barrier_semaphore()
    peers_t = [{"tensor": lax.rem(t + d, T)} for d in range(1, T)]
    peers_g = [
        {"dp": lax.rem(a + d, DP), "seq": lax.rem(s + e, S)}
        for d in range(DP)
        for e in range(S)
        if d or e
    ]
    for peer in peers_t + peers_g:
        pl.semaphore_signal(barrier, inc=1, device_id=peer, device_id_type=MESH)

    loads = [
        pltpu.make_async_copy(src, dst, in_sem.at[i])
        for i, (src, dst) in enumerate(
            [
                (hidden_h, hidden),
                (w_in_h, w_in),
                (mask_h, mask),
                (tokens_h, tokens),
                (embed_h, embed),
                (gain_h, gain),
                (w_head_h, w_head),
            ]
        )
    ]
    for load in loads:
        load.start()

    sends, seen = [], set()

    def got(copy):
        copy.wait_recv()
        seen.add(id(copy))

    def send(src, dst, ss, rs, peer):
        copy = pltpu.make_async_remote_copy(
            src_ref=src, dst_ref=dst, send_sem=ss, recv_sem=rs, device_id=peer, device_id_type=MESH
        )
        copy.start()
        sends.append(copy)
        return copy

    loads[0].wait()
    loads[1].wait()
    part = jnp.dot(hidden[...], w_in[...], preferred_element_type=F32).reshape(T, frames, width)
    ctx_send[...] = part.astype(BF16)
    ctx_own[...] = part
    loads[2].wait()
    mask_row = mask[...].astype(F32)
    cnt[...] = jnp.zeros(cnt.shape, F32) + jnp.sum(mask_row)
    pl.semaphore_wait(barrier, len(peers_t) + len(peers_g))
    ctx_copies = [
        send(ctx_send.at[lax.rem(t + d, T)], ctx_recv.at[d - 1], ctx_ss.at[d - 1], ctx_rs.at[d - 1],
             peers_t[d - 1])
        for d in range(1, T)
    ]
    cnt_copies = [
        send(cnt, cnt_recv.at[i], cnt_ss.at[i], cnt_rs.at[i], peer) for i, peer in enumerate(peers_g)
    ]

    loads[3].wait()
    spot = lax.broadcasted_iota(jnp.int32, (frames, nframes), 0) + t * frames
    here = lax.broadcasted_iota(jnp.int32, (frames, nframes), 1)
    mine = spot == here
    tok = tokens[...].astype(F32)
    lanes = lax.broadcasted_iota(jnp.int32, (frames, vocab), 1).astype(F32)
    hot = [
        jnp.sum(jnp.where(mine, tok[k : k + 1, :], 0.0), 1, keepdims=True) == lanes
        for k in range(steps)
    ]
    loads[4].wait()
    prev = jnp.concatenate([jnp.where(h, 1.0, 0.0).astype(BF16) for h in hot[:-1]], 0)
    gath[...] = jnp.dot(prev, embed[...], preferred_element_type=F32)
    mcol = jnp.sum(jnp.where(mine, mask_row, 0.0), 1, keepdims=True)
    loads[5].wait()
    loads[6].wait()
    gvec = gain[...]

    ctx = ctx_own[t]
    for d in range(1, T):
        got(ctx_copies[d - 1])
        ctx = ctx + ctx_recv[d - 1].astype(F32)
    ctx = ctx.astype(BF16).astype(F32)
    inputs = jnp.concatenate([ctx] * steps, 0) + jnp.concatenate(
        [jnp.zeros((frames, width), F32), gath[...]], 0
    )
    inverse = lax.rsqrt(jnp.mean(inputs * inputs, -1, keepdims=True) + 1e-06)
    normed = inputs * inverse
    flat = (normed * gvec).astype(BF16)
    scaled[...] = flat
    logits = jnp.dot(flat, w_head[...], preferred_element_type=F32)
    top = jnp.max(logits, -1, keepdims=True)
    powers = jnp.exp(logits - top)
    norm = jnp.sum(powers, -1, keepdims=True)
    total = top + jnp.log(norm)
    onehot = jnp.concatenate([jnp.where(h, 1.0, 0.0) for h in hot], 0)
    weights = jnp.concatenate([mcol] * steps, 0)
    nll = total - jnp.sum(logits * onehot, -1, keepdims=True)
    grads = ((powers * (1.0 / norm) - onehot) * weights).astype(BF16)
    gl[...] = grads

    chunk = width // DP
    order = []
    for j in range(DP - 1):
        up = jnp.where(j < a, j, j + 1)
        down = jnp.where(DP - 1 - j > a, DP - 1 - j, DP - 2 - j)
        order.append(jnp.where(2 * a < DP, down, up))
    order.append(a)
    h1, h2 = [], []

    def tensor_stage(j):
        acc = hs[j, :, s].astype(F32)
        for e in range(1, S):
            got(h1[j * (S - 1) + e - 1])
            acc = acc + r1[j, e - 1].astype(F32)
        s1[j] = acc.astype(BF16)
        for d in range(1, T):
            h2.append(
                send(s1.at[j, lax.rem(t + d, T)], r2.at[j, d - 1], h2_ss.at[j, d - 1],
                     h2_rs.at[j, d - 1], peers_t[d - 1])
            )

    lag = 1
    for j in range(DP):
        c = order[j]
        cols = scaled[:, pl.ds(pl.multiple_of(c * chunk, chunk), chunk)]
        term = lax.dot_general(
            cols, gl[...], (((0,), (0,)), ((), ())), preferred_element_type=F32
        )
        hs[j] = term.astype(BF16).reshape(T, S, piece, vocab)
        for e in range(1, S):
            h1.append(
                send(hs.at[j, :, lax.rem(s + e, S)], r1.at[j, e - 1], h1_ss.at[j, e - 1],
                     h1_rs.at[j, e - 1], {"seq": lax.rem(s + e, S)})
            )
        if j >= lag:
            tensor_stage(j - lag)
    for j in range(max(DP - lag, 0), DP):
        tensor_stage(j)
    ls1[...] = jnp.zeros(ls1.shape, F32) + jnp.sum(weights * nll)
    n = 0
    lc1 = []
    for e in range(1, S):
        lc1.append(send(ls1, ls1_r.at[e - 1], l_ss.at[n], l_rs.at[n], {"seq": lax.rem(s + e, S)}))
        n += 1

    lsum = ls1[...]
    for e in range(1, S):
        got(lc1[e - 1])
        lsum = lsum + ls1_r[e - 1]
    ls2[...] = lsum
    lc2 = []
    for d in range(1, T):
        lc2.append(send(ls2, ls2_r.at[d - 1], l_ss.at[n], l_rs.at[n], peers_t[d - 1]))
        n += 1

    grad_scaled = lax.dot_general(
        gl[...], w_head[...], (((1,), (1,)), ((), ())), preferred_element_type=F32
    )
    g = grad_scaled * gvec
    gi = inverse * (g - normed * jnp.mean(g * normed, -1, keepdims=True))
    gsum = gi[0:frames]
    for k in range(1, steps):
        gsum = gsum + gi[k * frames : (k + 1) * frames]
    gc[t] = gsum.astype(BF16)
    gc_copies = [
        send(gc.at[t], gc.at[t], gc_ss.at[d - 1], gc_rs.at[d - 1], peers_t[d - 1])
        for d in range(1, T)
    ]

    h3 = []
    for j in range(DP):
        acc = s1[j, t].astype(F32)
        for d in range(1, T):
            got(h2[j * (T - 1) + d - 1])
            acc = acc + r2[j, d - 1].astype(F32)
        if j < DP - 1:
            s2[j] = acc.astype(BF16)
            slot = lax.rem(order[j] - a + DP, DP) - 1
            h3.append(
                send(s2.at[j], r3.at[slot], h3_ss.at[j], h3_rs.at[slot], {"dp": order[j]})
            )
    lsum = ls2[...]
    for d in range(1, T):
        got(lc2[d - 1])
        lsum = lsum + ls2_r[d - 1]
    ls3[...] = lsum
    lc3 = []
    for d in range(1, DP):
        lc3.append(
            send(ls3, ls3_r.at[d - 1], l_ss.at[n], l_rs.at[n], {"dp": lax.rem(a + d, DP)})
        )
        n += 1
    total_mask = cnt[...]
    for i in range(len(peers_g)):
        got(cnt_copies[i])
        total_mask = total_mask + cnt_recv[i]
    share = 1.0 / (total_mask[0:1, 0:1] * steps)
    for d in range(1, T):
        got(gc_copies[d - 1])
    product = lax.dot_general(
        gc[...].reshape(nframes, width), w_in[...], (((1,), (1,)), ((), ())),
        preferred_element_type=F32,
    )
    gh_o[...] = (product * share).astype(BF16)

    for j in range(DP - 1):
        arrival = pltpu.make_async_remote_copy(
            src_ref=s2.at[j], dst_ref=r3.at[j], send_sem=h3_ss.at[j], recv_sem=h3_rs.at[j],
            device_id={"dp": lax.rem(a + 1, DP)}, device_id_type=MESH,
        )
        arrival.wait_recv()
        acc = acc + r3[j].astype(F32)
    acc = acc * share
    groups = vocab // 128
    for b in range(groups):
        head_o[pl.ds(b, piece, stride=groups), :] = acc[:, b * 128 : (b + 1) * 128]
    for d in range(1, DP):
        got(lc3[d - 1])
        lsum = lsum + ls3_r[d - 1]
    loss_o[...] = lsum[0:1, 0:1] * share
    for copy in sends:
        copy.wait_send()


def write_out(loss_i, head_i, gh_i, loss_o, head_o, gh_o, sem):
    copies = [
        pltpu.make_async_copy(src, dst, sem.at[i])
        for i, (src, dst) in enumerate([(gh_i, gh_o), (head_i, head_o), (loss_i, loss_o)])
    ]
    for copy in copies:
        copy.start()
    for copy in copies:
        copy.wait()


def per_device_kernel(hidden, w_in, embed, gain, w_head, tokens, frame_mask):
    DP, T, S = lax.axis_size("dp"), lax.axis_size("tensor"), lax.axis_size("seq")
    nframes, feats = hidden.shape
    steps = tokens.shape[1]
    frames = nframes // T
    width, vocab = w_head.shape
    rows = frames * steps
    piece = width // (DP * T * S)
    G = DP * S - 1
    V = pltpu.VMEM
    dma = pltpu.SemaphoreType.DMA
    scratch = [
        V(hidden.shape, BF16), V(w_in.shape, BF16), V(embed.shape, BF16), V((1, width), F32),
        V(w_head.shape, BF16), V((steps, nframes), jnp.int32), V((1, nframes), jnp.int32),
        V((T, frames, width), F32),
        V((T, frames, width), BF16),
        V((T - 1, frames, width), BF16),
        V((8, 128), F32),
        V((G, 8, 128), F32),
        V((rows - frames, width), F32),
        V((rows, width), BF16),
        V((rows, vocab), BF16),
        V((DP, T, S, piece, vocab), BF16),
        V((DP, S - 1, T, piece, vocab), BF16),
        V((DP, T, piece, vocab), BF16),
        V((DP, T - 1, piece, vocab), BF16),
        V((DP - 1, piece, vocab), BF16),
        V((DP - 1, piece, vocab), BF16),
        V((T, frames, width), BF16),
        V((8, 128), F32), V((S - 1, 8, 128), F32),
        V((8, 128), F32), V((T - 1, 8, 128), F32),
        V((8, 128), F32), V((DP - 1, 8, 128), F32),
        dma((7,)),
        dma((T - 1,)), dma((T - 1,)), dma((G,)), dma((G,)), dma((T - 1,)), dma((T - 1,)),
        dma((DP, S - 1)), dma((DP, S - 1)), dma((DP, T - 1)), dma((DP, T - 1)),
        dma((DP - 1,)), dma((DP - 1,)), dma((S + T + DP - 3,)), dma((S + T + DP - 3,)),
    ]
    shapes = (
        jax.ShapeDtypeStruct((1, 1), F32),
        jax.ShapeDtypeStruct((piece * vocab // 128, 128), F32),
        jax.ShapeDtypeStruct((nframes, feats), BF16),
    )
    vmem = pl.BlockSpec(memory_space=pltpu.VMEM)
    results = pl.pallas_call(
        functools.partial(kernel, (DP, T, S)),
        out_shape=shapes,
        in_specs=[pl.BlockSpec(memory_space=pltpu.HBM)] * 7,
        out_specs=(vmem, vmem, vmem),
        scratch_shapes=scratch,
        compiler_params=pltpu.CompilerParams(
            collective_id=0, has_side_effects=True, vmem_limit_bytes=40 << 20
        ),
        name="decode",
    )(*[pltpu.with_memory_space_constraint(x, pltpu.HBM) for x in (hidden, w_in, embed, gain.reshape(1, -1), w_head, tokens.T, frame_mask.reshape(1, -1))])
    loss, head, grad_hidden = pl.pallas_call(
        write_out,
        out_shape=shapes,
        in_specs=[pl.BlockSpec(memory_space=pl.ANY)] * 3,
        out_specs=(pl.BlockSpec(memory_space=pltpu.HBM),) * 3,
        scratch_shapes=[dma((3,))],
        compiler_params=pltpu.CompilerParams(vmem_limit_bytes=4 << 20),
        name="write_out",
    )(*results)
    return loss.reshape(()), head.reshape(-1), grad_hidden


def solution(mesh):
    def per_device(hidden, w_in, embed, gain, w_head, tokens, frame_mask):
        DP, T, S = mesh.shape["dp"], mesh.shape["tensor"], mesh.shape["seq"]
        width, vocab = w_head.shape
        fits = (
            width % (16 * DP * T * S) == 0
            and width % (128 * DP) == 0
            and vocab % 128 == 0
            and hidden.shape[0] % (16 * T) == 0
            and min(DP, T, S) > 1
        )
        run = per_device_kernel if fits else per_device_plain
        return run(hidden, w_in, embed, gain, w_head, tokens, frame_mask)

    placed = (
        P(("dp", "seq"), "tensor"),
        P("tensor", None),
        P(),
        P(),
        P(),
        P(("dp", "seq"), None),
        P(("dp", "seq")),
    )
    return jax.shard_map(
        per_device,
        mesh=mesh,
        in_specs=placed,
        out_specs=(P(), P(("dp", "tensor", "seq")), P(("dp", "seq"), "tensor")),
        check_vma=False,
    )
```
